256 devices in a mesh: rep: 16 (over y, z_lo), fsdp: 16 (over x, z_hi, core).
Axes of the slice: x: 4, y: 4, z: 8 (z_hi: 2, z_lo: 4; z = z_hi * 4 + z_lo), core: 2. Of those that a mesh axis runs over, the one named last changes fastest.
Arguments:
- gradients: bfloat16 [16, 16, 1024, 2048], P('rep', 'fsdp'), may hold values from -6 to 6
- momentum: float32 [16, 1024, 2048], P('rep', None, 'fsdp'), may hold values from -12 to 12
- master_weights: float32 [1024, 2048], P(None, 'fsdp'), may hold values from -0.125 to 0.125
Outputs:
- new_momentum: float32 [16, 1024, 2048], P('rep', None, 'fsdp')
- new_master: float32 [1024, 2048], P(None, 'fsdp')
- weights_full: bfloat16 [1024, 2048], replicated
The draws below stay inside these ranges and needn't reach their ends.
All inputs are finite; a program needn't handle non-finite values.
Results may differ from the reference program's by a relative error of at most 0.012.
Values may be sent and summed in bfloat16 or wider, within the bound.
No kernel may reach another device: no remote copies, remote signals or barrier semaphores. Data moves between devices by JAX's collectives and lax.ppermute only.
A program may use at most 128 MiB of HBM per device.

```python
import jax
import jax.numpy as jnp
from jax import lax

D = 2048
ROWS = 1024
GROUP = 128
BAND = 16
REPS = 16
SHARDS = 16


def with_spikes(array, rng, source, target, parts, factor):
    owner, partner = [(jnp.arange(array.shape[axis_at]) // (array.shape[axis_at] // parts)).reshape([-1 if axis == axis_at else 1 for axis in range(array.ndim)]) for axis_at in (source, target)]
    chosen = jax.random.permutation(rng, parts)[partner]
    strong = (owner == chosen) | (owner == (partner + parts // 2) % parts)
    return jnp.where(strong, factor * array, array)


def level_of(stream_key, extent, split, smallest, high):
    gain, own = 1.0, jax.random.fold_in(stream_key, 6)
    for position, parts in split:
        draws = jnp.exp(jax.random.uniform(jax.random.fold_in(own, position), (parts,), jnp.float32, smallest / len(split), high / len(split)))
        gain = gain * jnp.repeat(draws, extent[position] // parts).reshape([-1 if axis == position else 1 for axis in range(len(extent))])
    return gain


def normal_values(stream_key, dims, width, bound, pieces=(), kind=jnp.bfloat16):
    gain = level_of(stream_key, dims, pieces, -0.22, 0.18) if pieces else 1.0
    entries = jax.random.normal(stream_key, dims, jnp.float32) * width * gain
    return jnp.minimum(jnp.maximum(entries, -bound), bound).astype(kind)


def noise_with(stream_key, extent, scale, most, cuts, heavy, kind=jnp.bfloat16):
    entries = scale * jax.random.normal(stream_key, extent, jnp.float32)
    if cuts:
        entries = entries * level_of(stream_key, extent, cuts, -0.22, 0.18)
    return jnp.clip(with_spikes(entries, jax.random.fold_in(stream_key, 3), *heavy), -most, most).astype(kind)


def setup_inputs(seed: int = 0) -> dict:
    seeds = jax.random.split(jax.random.key(seed), 4)
    gradients = noise_with(seeds[0], (REPS, SHARDS, ROWS, D), 1.0, 6.0, ((0, 16), (1, 16)), (1, 3, 16, 2.0))
    momentum = normal_values(seeds[1], (REPS, ROWS, D), 2.0, 12.0, ((0, 16), (2, 16)), jnp.float32)
    master_weights = normal_values(seeds[2], (ROWS, D), D ** -0.5, 0.125, ((1, 16),), jnp.float32)
    return {"gradients": gradients, "momentum": momentum, "master_weights": master_weights}


momentum_decay = 0.9
step_size = 0.05

def cosine_rows():
    freq = jnp.arange(BAND, dtype=jnp.float32)[:, None]
    place = jnp.arange(GROUP, dtype=jnp.float32)[None, :]
    factor = jnp.where(freq == 0.0, jnp.sqrt(1.0 / GROUP), jnp.sqrt(2.0 / GROUP)).astype(jnp.float32)
    return (factor * jnp.cos(jnp.pi * (2.0 * place + 1.0) * freq / (2.0 * GROUP))).astype(jnp.float32)

def band_of(matrix):
    table = cosine_rows()
    blocks = matrix.reshape(matrix.shape[0] // GROUP, GROUP, matrix.shape[1] // GROUP, GROUP)
    return jnp.einsum('kr,arbc,lc->abkl', table, blocks, table, precision=lax.Precision.HIGHEST)

def spread_band(coeffs):
    table = cosine_rows()
    blocks = jnp.einsum('kr,abkl,lc->arbc', table, coeffs, table, precision=lax.Precision.HIGHEST)
    return blocks.reshape(coeffs.shape[0] * GROUP, coeffs.shape[1] * GROUP)

def one_replica(inputs):
    partial_grads, moment_old = inputs
    summed = lax.optimization_barrier(jnp.sum(partial_grads.astype(jnp.float32), axis=0))
    moment = momentum_decay * moment_old + summed
    band = band_of(moment)
    return (moment - spread_band(band), band)

def reference(gradients, momentum, master_weights):
    new_momentum, bands = lax.map(one_replica, (gradients, momentum))
    mean_band = lax.optimization_barrier(jnp.sum(bands, axis=0)) / REPS
    new_master = master_weights - step_size * spread_band(mean_band)
    return (new_momentum, new_master, new_master.astype(jnp.bfloat16))
```

```python
import functools

import jax
import jax.numpy as jnp
import numpy as np
from jax import lax
from jax.experimental import pallas as pl
from jax.experimental.pallas import tpu as pltpu
from jax.sharding import Mesh
from jax.sharding import PartitionSpec as P

GROUP = 128
BAND = 16
ROWS = 1024
HALF = 512
QUARTER = 256

momentum_decay = 0.9
step_size = 0.05
replicas = 16

bf16 = jnp.bfloat16
f32 = jnp.float32
HIGHEST = lax.Precision.HIGHEST

SWAP2 = [(0, 1), (1, 0)]
UP4 = [(i, (i + 1) % 4) for i in range(4)]
DOWN4 = [(i, (i + 3) % 4) for i in range(4)]
ACROSS4 = [(i, (i + 2) % 4) for i in range(4)]
EVEN4 = [(0, 1), (1, 0), (2, 3), (3, 2)]
ODD4 = [(1, 2), (2, 1), (3, 0), (0, 3)]
XOR2 = [(i, i ^ 2) for i in range(4)]
MIRROR8 = [(i, 7 - i) for i in range(8)]


def cosine_rows():
    freq = np.arange(BAND, dtype=np.float64)[:, None]
    place = np.arange(GROUP, dtype=np.float64)[None, :]
    factor = np.where(freq == 0.0, np.sqrt(1.0 / GROUP), np.sqrt(2.0 / GROUP))
    return factor * np.cos(np.pi * (2.0 * place + 1.0) * freq / (2.0 * GROUP))


def column_of(dx, gz, core):
    bx = lax.rem(lax.axis_index("x") + dx, 4)
    zh = lax.axis_index("zh")
    bz = zh if gz == 0 else 1 - zh
    return bx * 4 + bz * 2 + core


def slot_of(dx, gz):
    bx = lax.rem(lax.axis_index("x") + dx, 4)
    zh = lax.axis_index("zh")
    return bx * 2 + (zh if gz == 0 else 1 - zh)


def lanes(index):
    return pl.ds(pl.multiple_of(index * GROUP, GROUP), GROUP)


def gather_kernel(partner, g_ref, out_ref, sem):
    core = lax.axis_index("core")
    core = 1 - core if partner else core
    copies = []
    for gz in range(2):
        for dx in range(4):
            k = gz * 4 + dx
            copies.append(
                pltpu.make_async_copy(
                    g_ref.at[:, lanes(column_of(dx, gz, core))], out_ref.at[k], sem.at[k]
                )
            )
    for c in copies:
        c.start()
    for c in copies:
        c.wait()


def gather_blocks(g, partner):
    return pl.pallas_call(
        functools.partial(gather_kernel, partner),
        out_shape=jax.ShapeDtypeStruct((8, ROWS, GROUP), bf16),
        in_specs=[pl.BlockSpec(memory_space=pl.ANY)],
        out_specs=pl.BlockSpec(memory_space=pl.ANY),
        scratch_shapes=[pltpu.SemaphoreType.DMA((8,))],
    )(g)


def pair_sum_kernel(
    own_ref, other_ref, mom_ref, table_ref, rows_ref, up_ref, down_ref, keep_up_ref, keep_down_ref,
    own_out_ref, band_ref, acc_ref,
):
    lane_slot = lax.broadcasted_iota(jnp.int32, (GROUP, GROUP), 1) // BAND
    table = table_ref[...]
    zero = jnp.zeros_like(table)
    total = None
    for gz in range(2):
        for dx in range(4):
            k = gz * 4 + dx
            s = (own_ref[k].astype(f32) + other_ref[k].astype(f32)).astype(bf16)
            if dx == 0:
                own_out_ref[gz] = s
            elif dx == 1:
                keep_up_ref[gz] = s[:HALF]
                up_ref[gz, 1] = s[HALF:]
            elif dx == 2:
                up_ref[gz, 0] = s[:HALF]
                down_ref[gz, 0] = s[HALF:]
            else:
                down_ref[gz, 1] = s[:HALF]
                keep_down_ref[gz] = s[HALF:]
            placed = jnp.where(lane_slot == slot_of(dx, gz), table, zero)
            part = jnp.dot(s, placed.astype(bf16), preferred_element_type=f32)
            if k == 0:
                part += jnp.dot(momentum_decay * mom_ref[...], placed, preferred_element_type=f32)
                acc_ref[...] = part
            else:
                acc_ref[...] += part
    for a in range(ROWS // GROUP):
        band_ref[a * BAND : (a + 1) * BAND, :] = jnp.dot(
            rows_ref[...],
            acc_ref[a * GROUP : (a + 1) * GROUP, :],
            precision=HIGHEST,
            preferred_element_type=f32,
        )


def pair_sum(own, other, mom, table, rows):
    shapes = [
        jax.ShapeDtypeStruct((2, 2, HALF, GROUP), bf16),
        jax.ShapeDtypeStruct((2, 2, HALF, GROUP), bf16),
        jax.ShapeDtypeStruct((2, HALF, GROUP), bf16),
        jax.ShapeDtypeStruct((2, HALF, GROUP), bf16),
        jax.ShapeDtypeStruct((2, ROWS, GROUP), bf16),
        jax.ShapeDtypeStruct((ROWS // GROUP * BAND, GROUP), f32),
    ]
    return pl.pallas_call(
        pair_sum_kernel,
        out_shape=shapes,
        scratch_shapes=[pltpu.VMEM((ROWS, GROUP), f32)],
        compiler_params=pltpu.CompilerParams(vmem_limit_bytes=40 * 2**20),
    )(own, other, mom, table, rows)


def remaining_kernel(own_ref, near_ref, far_ref, z_ref, mom_ref, q_ref, out_ref):
    q = q_ref[...]
    for a in range(ROWS // GROUP):
        r = slice(a * GROUP, (a + 1) * GROUP)
        summed = own_ref[r].astype(f32) + near_ref[r].astype(f32)
        summed = summed + far_ref[r].astype(f32) + z_ref[r].astype(f32)
        moment = momentum_decay * mom_ref[r] + summed
        low = jnp.dot(moment, q, precision=HIGHEST, preferred_element_type=f32)
        low = jnp.dot(q, low, precision=HIGHEST, preferred_element_type=f32)
        out_ref[r] = moment - low


def remaining_of(own, near, far, z, mom, q):
    return pl.pallas_call(
        remaining_kernel,
        out_shape=jax.ShapeDtypeStruct((ROWS, GROUP), f32),
        compiler_params=pltpu.CompilerParams(vmem_limit_bytes=40 * 2**20),
    )(own, near, far, z, mom, q)


def weights_kernel(
    *refs,
):
    own, partner = refs[0:5], refs[5:10]
    band_refs = refs[10:12]
    master_ref, cols_ref, table_ref = refs[12:15]
    master_out, full_out = refs[15:17]
    update_ref, page_ref, sem = refs[17:20]
    core = lax.axis_index("core")
    y = lax.axis_index("y")
    copies = []
    wide = jnp.concatenate([table_ref[...]] * 8, axis=0)
    wide = jnp.concatenate([wide] * 8, axis=1)
    row_slot = lax.broadcasted_iota(jnp.int32, wide.shape, 0) // BAND
    lane_slot = lax.broadcasted_iota(jnp.int32, wide.shape, 1) // GROUP
    wide = jnp.where(row_slot == lane_slot, wide, jnp.zeros_like(wide)).astype(bf16)
    for step, dy in enumerate((0, 3, 1, 2)):
        quarter = lax.rem(y + dy, 4)
        if step >= 2:
            copies[step - 2].wait()
        page = step % 2
        for who in range(2):
            side = core if who == 0 else 1 - core
            pieces = own if who == 0 else partner
            for half in range(2):
                a = quarter * 2 + half
                coeffs = band_refs[who][pl.ds(pl.multiple_of(a * BAND, BAND), BAND), :]
                spread = jnp.dot(
                    cols_ref[...], coeffs, precision=HIGHEST, preferred_element_type=f32
                )
                update_ref[half * GROUP : (half + 1) * GROUP, :] = jnp.dot(
                    spread.astype(bf16), wide, preferred_element_type=f32
                )
            for dx in range(4):
                for gz in range(2):
                    if step < 3:
                        prior = pieces[step][dx, gz]
                    elif dx < 2:
                        prior = pieces[3][dx, gz]
                    else:
                        prior = pieces[4][dx - 2, gz]
                    new = prior.astype(f32) + update_ref[:, lanes(slot_of(dx, gz))]
                    page_ref[page, :, lanes(column_of(dx, gz, side))] = new.astype(bf16)
            if who == 0:
                rows = pl.ds(pl.multiple_of(quarter * QUARTER, QUARTER), QUARTER)
                master_out[rows, :] = master_ref[rows, :] + update_ref[:, lanes(slot_of(0, 0))]
        copy = pltpu.make_async_copy(
            page_ref.at[page],
            full_out.at[pl.ds(pl.multiple_of(quarter * QUARTER, QUARTER), QUARTER), :],
            sem.at[step],
        )
        copy.start()
        copies.append(copy)
    copies[2].wait()
    copies[3].wait()


def weights_of(own, partner, bands, master, cols, table):
    vmem = pl.BlockSpec(memory_space=pltpu.VMEM)
    return pl.pallas_call(
        weights_kernel,
        out_shape=[
            jax.ShapeDtypeStruct((ROWS, GROUP), f32),
            jax.ShapeDtypeStruct((ROWS, 16 * GROUP), bf16),
        ],
        in_specs=[vmem] * 15,
        out_specs=[vmem, pl.BlockSpec(memory_space=pl.ANY)],
        scratch_shapes=[
            pltpu.VMEM((QUARTER, 8 * GROUP), f32),
            pltpu.VMEM((2, QUARTER, 16 * GROUP), bf16),
            pltpu.SemaphoreType.DMA((4,)),
        ],
        compiler_params=pltpu.CompilerParams(vmem_limit_bytes=48 * 2**20),
    )(*own, *partner, *bands, master, cols, table)


def added(a, b):
    return (a.astype(f32) + b.astype(f32)).astype(bf16)


def local(gradients, momentum, master_weights):
    table = cosine_rows()
    g = gradients[0, 0]
    mom = momentum[0]

    sent = gather_blocks(g, True)
    other = lax.ppermute(sent, "core", SWAP2)
    own = gather_blocks(g, False)

    y = lax.axis_index("y")
    w0 = lax.dynamic_slice_in_dim(master_weights, y * QUARTER, QUARTER, 0).astype(bf16)
    wz = lax.ppermute(w0, ("zl", "zh"), MIRROR8)
    w1 = jnp.stack([w0, wz])
    w_right = lax.ppermute(w1, "x", DOWN4)
    w_left = lax.ppermute(w1, "x", UP4)
    w_far = lax.ppermute(w1, "x", ACROSS4)
    q0 = jnp.stack([w1, w_right, w_far, w_left])
    qm = lax.ppermute(q0, "y", UP4)
    qp = lax.ppermute(q0, "y", DOWN4)
    q2a = lax.ppermute(qm[:2], "y", UP4)
    q2b = lax.ppermute(qp[2:], "y", DOWN4)
    own_w = (q0, qm, qp, q2a, q2b)
    partner_w = tuple(lax.ppermute(p, "core", SWAP2) for p in own_w)

    up, down, keep_up, keep_down, mine, band = pair_sum(
        own,
        other,
        mom,
        jnp.asarray(np.tile(table.T, (1, 8)), f32),
        jnp.asarray(table, f32),
    )

    totals = {}
    for gz in (1, 0):
        from_left = lax.ppermute(up[gz], "x", UP4)
        from_right = lax.ppermute(down[gz], "x", DOWN4)
        last_left = lax.ppermute(added(keep_up[gz], from_left[0]), "x", UP4)
        last_right = lax.ppermute(added(keep_down[gz], from_right[0]), "x", DOWN4)
        near = jnp.concatenate([from_right[1], from_left[1]])
        far = jnp.concatenate([last_left, last_right])
        totals[gz] = (mine[gz], near, far)
    a, b, c = totals[1]
    z_send = (a.astype(f32) + b.astype(f32) + c.astype(f32)).astype(bf16)
    from_z = lax.ppermute(z_send, "zh", SWAP2)

    for axis, perm in (
        ("x", EVEN4),
        ("x", ODD4),
        ("y", EVEN4),
        ("y", ODD4),
        ("zl", EVEN4),
        ("zl", XOR2),
        (("zl", "zh"), MIRROR8),
    ):
        band = band + lax.ppermute(band, axis, perm)
    band = band * (-step_size / replicas)
    band_other = lax.ppermute(band, "core", SWAP2)

    new_momentum = remaining_of(
        *totals[0], from_z, mom, jnp.asarray(table.T @ table, f32)
    )
    new_master, weights_full = weights_of(
        own_w,
        partner_w,
        (band, band_other),
        master_weights,
        jnp.asarray(table.T, f32),
        jnp.asarray(table, f32),
    )
    return (new_momentum[None], new_master, weights_full)


def solution(mesh):
    fine = Mesh(mesh.devices.reshape(4, 4, 4, 2, 2), ("y", "zl", "x", "zh", "core"))
    rep, fsdp = ("y", "zl"), ("x", "zh", "core")
    return jax.shard_map(
        local,
        mesh=fine,
        in_specs=(P(rep, fsdp, None, None), P(rep, None, fsdp), P(None, fsdp)),
        out_specs=(P(rep, None, fsdp), P(None, fsdp), P()),
        check_vma=False,
    )
```

```python
import functools

import jax
import jax.numpy as jnp
import numpy as np
from jax import lax
from jax.experimental import pallas as pl
from jax.experimental.pallas import tpu as pltpu
from jax.sharding import Mesh
from jax.sharding import PartitionSpec as P

GROUP = 128
BAND = 16
ROWS = 1024
HALF = 512
QUARTER = 256

momentum_decay = 0.9
step_size = 0.05
replicas = 16

bf16 = jnp.bfloat16
f32 = jnp.float32
HIGHEST = lax.Precision.HIGHEST

SWAP2 = [(0, 1), (1, 0)]
UP4 = [(i, (i + 1) % 4) for i in range(4)]
DOWN4 = [(i, (i + 3) % 4) for i in range(4)]
ACROSS4 = [(i, (i + 2) % 4) for i in range(4)]
EVEN4 = [(0, 1), (1, 0), (2, 3), (3, 2)]
ODD4 = [(1, 2), (2, 1), (3, 0), (0, 3)]
XOR2 = [(i, i ^ 2) for i in range(4)]
CROSS8 = [(i, i ^ 5) for i in range(8)]
SPREAD8 = [(i, (i + 2) % 8) if i % 2 == 0 else (i, (i + 6) % 8) for i in range(8)]


def cosine_rows():
    freq = np.arange(BAND, dtype=np.float64)[:, None]
    place = np.arange(GROUP, dtype=np.float64)[None, :]
    factor = np.where(freq == 0.0, np.sqrt(1.0 / GROUP), np.sqrt(2.0 / GROUP))
    return factor * np.cos(np.pi * (2.0 * place + 1.0) * freq / (2.0 * GROUP))


def column_of(dx, gz, core):
    bx = lax.rem(lax.axis_index("x") + dx, 4)
    zh = lax.axis_index("zh")
    bz = zh if gz == 0 else 1 - zh
    return bx * 4 + bz * 2 + core


def slot_of(dx, gz):
    bx = lax.rem(lax.axis_index("x") + dx, 4)
    zh = lax.axis_index("zh")
    return bx * 2 + (zh if gz == 0 else 1 - zh)


def lanes(index):
    return pl.ds(pl.multiple_of(index * GROUP, GROUP), GROUP)


def split_kernel(g_ref, sent_ref, own_ref, page_ref, sem):
    core = lax.axis_index("core")
    copies = []
    for a in range(8):
        rows = slice(a * GROUP, (a + 1) * GROUP)
        copies.append(pltpu.make_async_copy(g_ref.at[rows, :], page_ref.at[rows, :], sem.at[a]))
    for c in copies:
        c.start()
    for a in range(8):
        rows = slice(a * GROUP, (a + 1) * GROUP)
        copies[a].wait()
        for gz in range(2):
            for dx in range(4):
                k = gz * 4 + dx
                sent_ref[k, rows] = page_ref[rows, lanes(column_of(dx, gz, 1 - core))]
                own_ref[k, rows] = page_ref[rows, lanes(column_of(dx, gz, core))]


def split_blocks(g):
    blocks = jax.ShapeDtypeStruct((8, ROWS, GROUP), bf16)
    return pl.pallas_call(
        split_kernel,
        out_shape=[blocks, blocks],
        in_specs=[pl.BlockSpec(memory_space=pltpu.HBM)],
        out_specs=[pl.BlockSpec(memory_space=pltpu.VMEM)] * 2,
        scratch_shapes=[pltpu.VMEM((ROWS, 16 * GROUP), bf16), pltpu.SemaphoreType.DMA((8,))],
        compiler_params=pltpu.CompilerParams(vmem_limit_bytes=12 * 2**20),
    )(g)


def pair_sum_kernel(
    own_ref, other_ref, mom_ref, table_ref, rows_ref, up_ref, down_ref, keep_up_ref, keep_down_ref,
    mine_ref, band_ref, acc_ref,
):
    lane_slot = lax.broadcasted_iota(jnp.int32, (GROUP, GROUP), 1) // BAND
    table = table_ref[...]
    zero = jnp.zeros_like(table)
    for gz in range(2):
        for dx in range(4):
            k = gz * 4 + dx
            s = (own_ref[k].astype(f32) + other_ref[k].astype(f32)).astype(bf16)
            if dx == 0:
                mine_ref[gz] = s
            elif dx == 1:
                keep_up_ref[gz] = s[:HALF]
                up_ref[gz, 1] = s[HALF:]
            elif dx == 2:
                up_ref[gz, 0] = s[:HALF]
                down_ref[gz, 0] = s[HALF:]
            else:
                down_ref[gz, 1] = s[:HALF]
                keep_down_ref[gz] = s[HALF:]
            placed = jnp.where(lane_slot == slot_of(dx, gz), table, zero)
            part = jnp.dot(s, placed.astype(bf16), preferred_element_type=f32)
            if k == 0:
                acc_ref[...] = part + jnp.dot(
                    momentum_decay * mom_ref[...], placed, preferred_element_type=f32
                )
            else:
                acc_ref[...] += part
    for a in range(ROWS // GROUP):
        band_ref[a * BAND : (a + 1) * BAND, :] = jnp.dot(
            rows_ref[...],
            acc_ref[a * GROUP : (a + 1) * GROUP, :],
            precision=HIGHEST,
            preferred_element_type=f32,
        )


def pair_sum(own, other, mom, table, rows):
    shapes = [(2, 2, HALF, GROUP)] * 2 + [(2, HALF, GROUP)] * 2 + [(2, ROWS, GROUP)]
    shapes = [jax.ShapeDtypeStruct(shape, bf16) for shape in shapes]
    shapes.append(jax.ShapeDtypeStruct((ROWS // GROUP * BAND, GROUP), f32))
    vmem = pl.BlockSpec(memory_space=pltpu.VMEM)
    return pl.pallas_call(
        pair_sum_kernel,
        out_shape=shapes,
        in_specs=[vmem] * 5,
        out_specs=[vmem] * 6,
        scratch_shapes=[pltpu.VMEM((ROWS, GROUP), f32)],
        compiler_params=pltpu.CompilerParams(vmem_limit_bytes=16 * 2**20),
    )(own, other, mom, table, rows)


def small_call(kernel, shapes, *args):
    vmem = pl.BlockSpec(memory_space=pltpu.VMEM)
    return pl.pallas_call(
        kernel,
        out_shape=shapes,
        in_specs=[vmem] * len(args),
        out_specs=jax.tree.map(lambda _: vmem, shapes),
        compiler_params=pltpu.CompilerParams(vmem_limit_bytes=8 * 2**20),
    )(*args)


def join_kernel(first_ref, second_ref, out_ref):
    half = first_ref.shape[0]
    out_ref[:half] = first_ref[...]
    out_ref[half:] = second_ref[...]


def joined(first, second):
    shape = (2 * first.shape[0], *first.shape[1:])
    return small_call(join_kernel, jax.ShapeDtypeStruct(shape, first.dtype), first, second)


def cast_kernel(master_ref, out_ref):
    y = lax.axis_index("y")
    out_ref[0] = master_ref[pl.ds(pl.multiple_of(y * QUARTER, QUARTER), QUARTER), :].astype(bf16)


def pass_on_kernel(keep_up_ref, keep_down_ref, left_ref, right_ref, up_ref, down_ref):
    for gz in range(2):
        up_ref[gz] = (keep_up_ref[gz].astype(f32) + left_ref[gz, 0].astype(f32)).astype(bf16)
        down_ref[gz] = (keep_down_ref[gz].astype(f32) + right_ref[gz, 0].astype(f32)).astype(bf16)


def x_total(mine_ref, left_ref, right_ref, last_left_ref, last_right_ref, gz, a):
    r = slice(a * GROUP, (a + 1) * GROUP)
    h = slice(a % 4 * GROUP, (a % 4 + 1) * GROUP)
    direct, passed = (right_ref, last_left_ref) if a < 4 else (left_ref, last_right_ref)
    total = mine_ref[gz, r].astype(f32) + direct[gz, 1, h].astype(f32)
    return total + passed[gz, h].astype(f32)


def z_send_kernel(*refs):
    for a in range(ROWS // GROUP):
        refs[5][a * GROUP : (a + 1) * GROUP] = x_total(*refs[:5], 1, a).astype(bf16)


def remaining_kernel(*refs):
    z_ref, mom_ref, q_ref, out_ref = refs[5:]
    q = q_ref[...]
    for a in range(ROWS // GROUP):
        r = slice(a * GROUP, (a + 1) * GROUP)
        summed = x_total(*refs[:5], 0, a) + z_ref[r].astype(f32)
        moment = momentum_decay * mom_ref[r] + summed
        low = jnp.dot(moment, q, precision=HIGHEST, preferred_element_type=f32)
        low = jnp.dot(q, low, precision=HIGHEST, preferred_element_type=f32)
        out_ref[r] = moment - low


def gathered_x(j):
    x = lax.axis_index("x")
    if j >= 2:
        x = lax.rem(x + 3 - 2 * lax.rem(x, 2), 4)
        x = lax.rem(x + 4, 4)
    return x if j % 2 == 0 else x + 1 - 2 * lax.rem(x, 2)


def weights_kernel(*refs):
    quarter_ref, near_ref, near_other_ref, far_ref, far_other_ref = refs[0:5]
    band_refs = refs[5:7]
    master_ref, cols_ref, table_ref = refs[7:10]
    master_out, full_out = refs[10:12]
    spread_ref, page_ref, sem = refs[12:15]
    core = lax.axis_index("core")
    y = lax.axis_index("y")
    zh = lax.axis_index("zh")

    coeffs = jnp.concatenate([band_refs[0][...], band_refs[1][...]], axis=1)
    spread_ref[...] = jnp.dot(
        cols_ref[...], coeffs.astype(bf16), preferred_element_type=f32
    ).astype(bf16)

    row_slot = lax.broadcasted_iota(jnp.int32, (GROUP, GROUP), 0) // BAND
    table = table_ref[...]
    zero = jnp.zeros_like(table)
    places = []
    for j in range(4):
        for gz in range(2):
            bx, bz = gathered_x(j), (zh if gz == 0 else 1 - zh)
            slot = bx * 2 + bz
            places.append((j, gz, bx * 4 + bz * 2))
            wide_part = jnp.where(row_slot == slot, table, zero).astype(bf16)
            wide = wide_part if j + gz == 0 else jnp.concatenate([wide, wide_part], axis=1)

    copies = []
    for step, dy in enumerate((0, 3 - 2 * core, 1 + 2 * core, 2)):
        quarter = lax.rem(y + dy, 4)
        rows = pl.ds(pl.multiple_of(quarter * QUARTER, QUARTER), QUARTER)
        for who in range(2):
            side = core if who == 0 else 1 - core
            update = jnp.dot(
                spread_ref[rows, who * GROUP : (who + 1) * GROUP],
                wide,
                preferred_element_type=f32,
            )
            for j, gz, column in places:
                k = j * 2 + gz
                if step == 0:
                    prior = quarter_ref[who * 8 + k]
                elif step == 1:
                    prior = near_ref[who * 8 + k]
                elif step == 2:
                    prior = near_other_ref[(1 - who) * 8 + k]
                else:
                    prior = far_ref[k] if who == 0 else far_other_ref[k]
                part = update[:, k * GROUP : (k + 1) * GROUP]
                page_ref[step, :, lanes(column + side)] = (prior.astype(f32) + part).astype(bf16)
                if who == 0 and k == 0:
                    master_out[rows, :] = master_ref[rows, :] + part
        copy = pltpu.make_async_copy(page_ref.at[step], full_out.at[rows, :], sem.at[step])
        copy.start()
        copies.append(copy)
    for copy in copies:
        copy.wait()


def weights_of(pieces, bands, master, cols, table):
    vmem = pl.BlockSpec(memory_space=pltpu.VMEM)
    return pl.pallas_call(
        weights_kernel,
        out_shape=[
            jax.ShapeDtypeStruct((ROWS, GROUP), f32),
            jax.ShapeDtypeStruct((ROWS, 16 * GROUP), bf16),
        ],
        in_specs=[vmem] * 10,
        out_specs=[vmem, pl.BlockSpec(memory_space=pl.ANY)],
        scratch_shapes=[
            pltpu.VMEM((ROWS, 2 * GROUP), bf16),
            pltpu.VMEM((4, QUARTER, 16 * GROUP), bf16),
            pltpu.SemaphoreType.DMA((4,)),
        ],
        compiler_params=pltpu.CompilerParams(vmem_limit_bytes=20 * 2**20),
    )(*pieces, *bands, master, cols, table)


def send(array, axis, perm):
    return lax.ppermute(array, axis, perm)


together = lax.optimization_barrier


def local(gradients, momentum, master_weights):
    table = cosine_rows()
    mom = momentum[0]
    half = (ROWS, GROUP)
    z = ("zl", "zh")

    sent, own = split_blocks(gradients[0, 0])
    other = send(sent, "core", SWAP2)
    w0 = small_call(
        cast_kernel, jax.ShapeDtypeStruct((1, QUARTER, GROUP), bf16), master_weights
    )
    wz = send(w0, z, CROSS8)
    up, down, keep_up, keep_down, mine, band = pair_sum(
        own,
        other,
        mom,
        jnp.asarray(np.tile(table.T, (1, 8)), f32),
        jnp.asarray(table, f32),
    )

    band, up, down, w0, wz = together((band, up, down, w0, wz))
    got = send(band, "y", EVEN4)
    left = send(up, "x", UP4)
    right = send(down, "x", DOWN4)
    w1 = joined(w0, wz)
    wx = send(w1, "x", EVEN4)

    band, w1, wx = together((band + got, w1, wx))
    got = send(band, "y", ODD4)
    w2 = joined(w1, wx)
    wx = send(w2, "x", ODD4)

    band, w2, wx = together((band + got, w2, wx))
    got = send(band, "zl", EVEN4)
    w4 = joined(w2, wx)
    wc = send(w4, "core", SWAP2)

    band, w4, wc, left, right = together((band + got, w4, wc, left, right))
    got = send(band, "zl", XOR2)
    quarter = joined(w4, wc)
    near = send(quarter, ("y", "core"), SPREAD8)
    passed = jax.ShapeDtypeStruct((2, HALF, GROUP), bf16)
    up, down = small_call(pass_on_kernel, [passed] * 2, keep_up, keep_down, left, right)
    last_left = send(up, "x", UP4)
    last_right = send(down, "x", DOWN4)

    band = band + got
    got = send(band, z, CROSS8)

    band, last_left, last_right = together((band + got, last_left, last_right))
    got = send(band, "x", EVEN4)
    parts = (mine, left, right, last_left, last_right)
    z_send = small_call(z_send_kernel, jax.ShapeDtypeStruct(half, bf16), *parts)
    from_z = send(z_send, "zh", SWAP2)

    band, near = together((band + got, near))
    got = send(band, "x", ODD4)
    far = send(near[:8], ("y", "core"), SPREAD8)
    near_other = send(near, "core", SWAP2)

    band, far = together(((band + got) * (-step_size / replicas), far))
    band_other = send(band, "core", SWAP2)
    far_other = send(far, "core", SWAP2)

    new_momentum = small_call(
        remaining_kernel,
        jax.ShapeDtypeStruct(half, f32),
        *parts,
        from_z,
        mom,
        jnp.asarray(table.T @ table, f32),
    )
    new_master, weights_full = weights_of(
        (quarter, near, near_other, far, far_other),
        (band, band_other),
        master_weights,
        jnp.asarray(np.kron(np.eye(8), table.T), bf16),
        jnp.asarray(np.tile(table, (8, 1)), f32),
    )
    return (new_momentum[None], new_master, weights_full)


def solution(mesh):
    fine = Mesh(mesh.devices.reshape(4, 4, 4, 2, 2), ("y", "zl", "x", "zh", "core"))
    rep, fsdp = ("y", "zl"), ("x", "zh", "core")
    return jax.shard_map(
        local,
        mesh=fine,
        in_specs=(P(rep, fsdp, None, None), P(rep, None, fsdp), P(None, fsdp)),
        out_specs=(P(rep, None, fsdp), P(None, fsdp), P()),
        check_vma=False,
    )
```

```python
import functools

import jax
import jax.numpy as jnp
import numpy as np
from jax import lax
from jax.experimental import pallas as pl
from jax.experimental.pallas import tpu as pltpu
from jax.sharding import Mesh
from jax.sharding import PartitionSpec as P

GROUP = 128
BAND = 16
ROWS = 1024
HALF = 512
QUARTER = 256

momentum_decay = 0.9
step_size = 0.05
replicas = 16

bf16 = jnp.bfloat16
f32 = jnp.float32
HIGHEST = lax.Precision.HIGHEST

SWAP2 = [(0, 1), (1, 0)]
UP4 = [(i, (i + 1) % 4) for i in range(4)]
DOWN4 = [(i, (i + 3) % 4) for i in range(4)]
ACROSS4 = [(i, (i + 2) % 4) for i in range(4)]
EVEN4 = [(0, 1), (1, 0), (2, 3), (3, 2)]
ODD4 = [(1, 2), (2, 1), (3, 0), (0, 3)]
XOR2 = [(i, i ^ 2) for i in range(4)]
CROSS8 = [(i, i ^ 5) for i in range(8)]
SPREAD8 = [(i, (i + 2) % 8) if i % 2 == 0 else (i, (i + 6) % 8) for i in range(8)]


def cosine_rows():
    freq = np.arange(BAND, dtype=np.float64)[:, None]
    place = np.arange(GROUP, dtype=np.float64)[None, :]
    factor = np.where(freq == 0.0, np.sqrt(1.0 / GROUP), np.sqrt(2.0 / GROUP))
    return factor * np.cos(np.pi * (2.0 * place + 1.0) * freq / (2.0 * GROUP))


def column_of(dx, gz, core):
    bx = lax.rem(lax.axis_index("x") + dx, 4)
    zh = lax.axis_index("zh")
    bz = zh if gz == 0 else 1 - zh
    return bx * 4 + bz * 2 + core


def slot_of(dx, gz):
    bx = lax.rem(lax.axis_index("x") + dx, 4)
    zh = lax.axis_index("zh")
    return bx * 2 + (zh if gz == 0 else 1 - zh)


def lanes(index):
    return pl.ds(pl.multiple_of(index * GROUP, GROUP), GROUP)


def split_kernel(g_ref, sent_ref, own_ref):
    core = lax.axis_index("core")
    for gz in range(2):
        for dx in range(4):
            k = gz * 4 + dx
            sent_ref[k] = g_ref[:, lanes(column_of(dx, gz, 1 - core))]
            own_ref[k] = g_ref[:, lanes(column_of(dx, gz, core))]


def split_blocks(g):
    blocks = jax.ShapeDtypeStruct((8, ROWS, GROUP), bf16)
    return pl.pallas_call(
        split_kernel,
        out_shape=[blocks, blocks],
        in_specs=[pl.BlockSpec(memory_space=pltpu.VMEM)],
        out_specs=[pl.BlockSpec(memory_space=pltpu.VMEM)] * 2,
        compiler_params=pltpu.CompilerParams(vmem_limit_bytes=12 * 2**20),
    )(g)


def pair_sum_kernel(
    own_ref, other_ref, mom_ref, table_ref, rows_ref, w0_ref, wz_ref, up_ref, down_ref,
    keep_up_ref, keep_down_ref, mine_ref, band_ref, acc_ref,
):
    for ref in (up_ref, down_ref):
        ref[4, :QUARTER] = w0_ref[...]
        ref[4, QUARTER:] = wz_ref[...]
    lane_slot = lax.broadcasted_iota(jnp.int32, (GROUP, GROUP), 1) // BAND
    table = table_ref[...]
    zero = jnp.zeros_like(table)
    for gz in range(2):
        for dx in range(4):
            k = gz * 4 + dx
            s = (own_ref[k].astype(f32) + other_ref[k].astype(f32)).astype(bf16)
            if dx == 0:
                mine_ref[gz] = s
            elif dx == 1:
                keep_up_ref[gz] = s[:HALF]
                up_ref[gz * 2 + 1] = s[HALF:]
            elif dx == 2:
                up_ref[gz * 2] = s[:HALF]
                down_ref[gz * 2] = s[HALF:]
            else:
                down_ref[gz * 2 + 1] = s[:HALF]
                keep_down_ref[gz] = s[HALF:]
            placed = jnp.where(lane_slot == slot_of(dx, gz), table, zero)
            part = jnp.dot(s, placed.astype(bf16), preferred_element_type=f32)
            if k == 0:
                acc_ref[...] = part + jnp.dot(
                    momentum_decay * mom_ref[...], placed, preferred_element_type=f32
                )
            else:
                acc_ref[...] += part
    for a in range(ROWS // GROUP):
        band_ref[a * BAND : (a + 1) * BAND, :] = jnp.dot(
            rows_ref[...],
            acc_ref[a * GROUP : (a + 1) * GROUP, :],
            precision=HIGHEST,
            preferred_element_type=f32,
        )


def pair_sum(*args):
    shapes = [(5, HALF, GROUP)] * 2 + [(2, HALF, GROUP)] * 2 + [(2, ROWS, GROUP)]
    shapes = [jax.ShapeDtypeStruct(shape, bf16) for shape in shapes]
    shapes.append(jax.ShapeDtypeStruct((ROWS // GROUP * BAND, GROUP), f32))
    vmem = pl.BlockSpec(memory_space=pltpu.VMEM)
    return pl.pallas_call(
        pair_sum_kernel,
        out_shape=shapes,
        in_specs=[vmem] * 7,
        out_specs=[vmem] * 6,
        scratch_shapes=[pltpu.VMEM((ROWS, GROUP), f32)],
        compiler_params=pltpu.CompilerParams(vmem_limit_bytes=16 * 2**20),
    )(*args)


def small_call(kernel, shapes, *args):
    vmem = pl.BlockSpec(memory_space=pltpu.VMEM)
    return pl.pallas_call(
        kernel,
        out_shape=shapes,
        in_specs=[vmem] * len(args),
        out_specs=jax.tree.map(lambda _: vmem, shapes),
        compiler_params=pltpu.CompilerParams(vmem_limit_bytes=8 * 2**20),
    )(*args)


def join_kernel(first_ref, second_ref, out_ref):
    half = first_ref.shape[0]
    out_ref[:half] = first_ref[...]
    out_ref[half:] = second_ref[...]


def joined(first, second):
    shape = (2 * first.shape[0], *first.shape[1:])
    return small_call(join_kernel, jax.ShapeDtypeStruct(shape, first.dtype), first, second)


def cast_kernel(master_ref, out_ref):
    y = lax.axis_index("y")
    out_ref[...] = master_ref[pl.ds(pl.multiple_of(y * QUARTER, QUARTER), QUARTER), :].astype(bf16)


def pass_on_kernel(keep_up_ref, keep_down_ref, left_ref, right_ref, up_ref, down_ref):
    for gz in range(2):
        r = slice(gz * HALF, (gz + 1) * HALF)
        up_ref[r] = (keep_up_ref[gz].astype(f32) + left_ref[gz * 2].astype(f32)).astype(bf16)
        down_ref[r] = (keep_down_ref[gz].astype(f32) + right_ref[gz * 2].astype(f32)).astype(bf16)
    up_ref[2 * HALF :] = left_ref[4, :QUARTER]
    down_ref[2 * HALF :] = right_ref[4, QUARTER:]


def collect_kernel(w0_ref, wz_ref, left_ref, right_ref, last_left_ref, last_right_ref, out_ref):
    out_ref[0] = w0_ref[...]
    out_ref[1] = left_ref[4, :QUARTER]
    out_ref[2] = right_ref[4, :QUARTER]
    out_ref[3] = last_left_ref[2 * HALF :]
    out_ref[4] = wz_ref[...]
    out_ref[5] = left_ref[4, QUARTER:]
    out_ref[6] = right_ref[4, QUARTER:]
    out_ref[7] = last_right_ref[2 * HALF :]


def x_total(mine_ref, left_ref, right_ref, last_left_ref, last_right_ref, gz, a):
    r = slice(a * GROUP, (a + 1) * GROUP)
    h = slice(a % 4 * GROUP, (a % 4 + 1) * GROUP)
    p = slice(gz * HALF + a % 4 * GROUP, gz * HALF + (a % 4 + 1) * GROUP)
    direct, passed = (right_ref, last_left_ref) if a < 4 else (left_ref, last_right_ref)
    total = mine_ref[gz, r].astype(f32) + direct[gz * 2 + 1, h].astype(f32)
    return total + passed[p].astype(f32)


def z_send_kernel(*refs):
    for a in range(ROWS // GROUP):
        refs[5][a * GROUP : (a + 1) * GROUP] = x_total(*refs[:5], 1, a).astype(bf16)


def remaining_kernel(*refs):
    z_ref, mom_ref, q_ref, out_ref = refs[5:]
    q = q_ref[...]
    for a in range(ROWS // GROUP):
        r = slice(a * GROUP, (a + 1) * GROUP)
        summed = x_total(*refs[:5], 0, a) + z_ref[r].astype(f32)
        moment = momentum_decay * mom_ref[r] + summed
        low = jnp.dot(moment, q, precision=HIGHEST, preferred_element_type=f32)
        low = jnp.dot(q, low, precision=HIGHEST, preferred_element_type=f32)
        out_ref[r] = moment - low


def gathered_x(j):
    return lax.rem(lax.axis_index("x") + (0, 3, 1, 2)[j], 4)


def columns_side(table_ref):
    zh = lax.axis_index("zh")
    row_slot = lax.broadcasted_iota(jnp.int32, (GROUP, GROUP), 0) // BAND
    table = table_ref[...]
    zero = jnp.zeros_like(table)
    columns = []
    wide = []
    for gz in range(2):
        for j in range(4):
            bx, bz = gathered_x(j), (zh if gz == 0 else 1 - zh)
            columns.append(bx * 4 + bz * 2)
            wide.append(jnp.where(row_slot == bx * 2 + bz, table, zero).astype(bf16))
    return jnp.concatenate(wide, axis=1), columns


def update_quarter(dy, pieces, spread_ref, wide, columns, page_ref, full_out, sem):
    core = lax.axis_index("core")
    quarter = lax.rem(lax.axis_index("y") + dy, 4)
    rows = pl.ds(pl.multiple_of(quarter * QUARTER, QUARTER), QUARTER)
    for who in range(2):
        side = core if who == 0 else 1 - core
        update = jnp.dot(
            spread_ref[rows, who * GROUP : (who + 1) * GROUP],
            wide,
            preferred_element_type=f32,
        )
        for k, column in enumerate(columns):
            part = update[:, k * GROUP : (k + 1) * GROUP]
            new = pieces[who][k].astype(f32) + part
            page_ref[:, lanes(column + side)] = new.astype(bf16)
    copy = pltpu.make_async_copy(page_ref, full_out.at[rows, :], sem)
    copy.start()
    return copy


def first_weights_kernel(
    quarter_ref, near_ref, near_other_ref, band_ref, band_other_ref, master_ref, cols_ref,
    table_ref, master_out, full_out, spread_ref, page_ref, sem,
):
    core = lax.axis_index("core")
    wide, columns = columns_side(table_ref)
    coeffs = jnp.concatenate([band_ref[...], band_other_ref[...]], axis=1)
    spread_ref[...] = jnp.dot(
        cols_ref[...], coeffs.astype(bf16), preferred_element_type=f32
    ).astype(bf16)
    low, high = slice(0, 8), slice(8, 16)
    copies = []
    for step, (dy, ref, parts) in enumerate(
        (
            (0, quarter_ref, (low, high)),
            (3 - 2 * core, near_ref, (low, high)),
            (1 + 2 * core, near_other_ref, (high, low)),
        )
    ):
        pieces = tuple(ref.at[part] for part in parts)
        copies.append(
            update_quarter(
                dy, pieces, spread_ref, wide, columns, page_ref.at[step], full_out, sem.at[step]
            )
        )
    master_out[...] = master_ref[...] + jnp.dot(
        spread_ref[:, :GROUP], wide[:, :GROUP], preferred_element_type=f32
    )
    for copy in copies:
        copy.wait()


def last_weights_kernel(
    far_ref, far_other_ref, spread_ref, table_ref, started_ref, full_out, page_ref, sem
):
    del started_ref
    wide, columns = columns_side(table_ref)
    update_quarter(
        2, (far_ref, far_other_ref), spread_ref, wide, columns, page_ref, full_out, sem
    ).wait()


def weights_of(quarters, last_quarter, bands, master, cols, table):
    vmem = pl.BlockSpec(memory_space=pltpu.VMEM)
    anywhere = pl.BlockSpec(memory_space=pl.ANY)
    full = jax.ShapeDtypeStruct((ROWS, 16 * GROUP), bf16)
    new_master, started, spread = pl.pallas_call(
        first_weights_kernel,
        out_shape=[
            jax.ShapeDtypeStruct((ROWS, GROUP), f32),
            full,
            jax.ShapeDtypeStruct((ROWS, 2 * GROUP), bf16),
        ],
        in_specs=[vmem] * 8,
        out_specs=[vmem, anywhere, vmem],
        scratch_shapes=[
            pltpu.VMEM((3, QUARTER, 16 * GROUP), bf16),
            pltpu.SemaphoreType.DMA((3,)),
        ],
        compiler_params=pltpu.CompilerParams(vmem_limit_bytes=20 * 2**20),
    )(*quarters, *bands, master, cols, table)
    weights_full = pl.pallas_call(
        last_weights_kernel,
        out_shape=full,
        in_specs=[vmem] * 4 + [anywhere],
        out_specs=anywhere,
        input_output_aliases={4: 0},
        scratch_shapes=[
            pltpu.VMEM((QUARTER, 16 * GROUP), bf16),
            pltpu.SemaphoreType.DMA,
        ],
        compiler_params=pltpu.CompilerParams(vmem_limit_bytes=12 * 2**20),
    )(*last_quarter, spread, table, started)
    return new_master, weights_full


def send(array, axis, perm):
    return lax.ppermute(array, axis, perm)


together = lax.optimization_barrier


def local(gradients, momentum, master_weights):
    table = cosine_rows()
    mom = momentum[0]
    half = (ROWS, GROUP)
    z = ("zl", "zh")

    sent, own = split_blocks(gradients[0, 0])
    other = send(sent, "core", SWAP2)
    w0 = small_call(cast_kernel, jax.ShapeDtypeStruct((QUARTER, GROUP), bf16), master_weights)
    wz = send(w0, z, CROSS8)
    up, down, keep_up, keep_down, mine, band = pair_sum(
        own,
        other,
        mom,
        jnp.asarray(np.tile(table.T, (1, 8)), f32),
        jnp.asarray(table, f32),
        w0,
        wz,
    )

    got = send(band, "zl", EVEN4)
    left = send(up, "x", UP4)
    right = send(down, "x", DOWN4)

    band = band + got
    got = send(band, "zl", XOR2)

    band = band + got
    got = send(band, z, CROSS8)

    band, left, right = together((band + got, left, right))
    got = send(band, "y", EVEN4)
    passed = jax.ShapeDtypeStruct((2 * HALF + QUARTER, GROUP), bf16)
    up, down = small_call(pass_on_kernel, [passed] * 2, keep_up, keep_down, left, right)
    last_left = send(up, "x", UP4)
    last_right = send(down, "x", DOWN4)

    band, last_left, last_right = together((band + got, last_left, last_right))
    got = send(band, "y", ODD4)
    parts = (mine, left, right, last_left, last_right)
    z_send = small_call(z_send_kernel, jax.ShapeDtypeStruct(half, bf16), *parts)
    from_z = send(z_send, "zh", SWAP2)
    eighth = small_call(
        collect_kernel, jax.ShapeDtypeStruct((8, QUARTER, GROUP), bf16), w0, wz, *parts[1:]
    )
    wc = send(eighth, "core", SWAP2)

    band, eighth, wc = together((band + got, eighth, wc))
    got = send(band, "x", EVEN4)
    quarter = joined(eighth, wc)
    near = send(quarter, ("y", "core"), SPREAD8)

    band, from_z, near = together((band + got, from_z, near))
    got = send(band, "x", ODD4)
    far = send(near[:8], ("y", "core"), SPREAD8)
    near_other = send(near, "core", SWAP2)
    new_momentum = small_call(
        remaining_kernel,
        jax.ShapeDtypeStruct(half, f32),
        *parts,
        from_z,
        mom,
        jnp.asarray(table.T @ table, f32),
    )

    band = (band + got) * (-step_size / replicas)
    band, new_momentum, near_other = together((band, new_momentum, near_other))
    band_other = send(band, "core", SWAP2)

    band, band_other, far = together((band, band_other, far))
    far_other = send(far, "core", SWAP2)
    new_master, weights_full = weights_of(
        (quarter, near, near_other),
        (far, far_other),
        (band, band_other),
        master_weights,
        jnp.asarray(np.kron(np.eye(8), table.T), bf16),
        jnp.asarray(np.tile(table, (8, 1)), f32),
    )
    return (new_momentum[None], new_master, weights_full)


def solution(mesh):
    fine = Mesh(mesh.devices.reshape(4, 4, 4, 2, 2), ("y", "zl", "x", "zh", "core"))
    rep, fsdp = ("y", "zl"), ("x", "zh", "core")
    return jax.shard_map(
        local,
        mesh=fine,
        in_specs=(P(rep, fsdp, None, None), P(rep, None, fsdp), P(None, fsdp)),
        out_specs=(P(rep, None, fsdp), P(None, fsdp), P()),
        check_vma=False,
    )
```

```python
import functools

import jax
import jax.numpy as jnp
import numpy as np
from jax import lax
from jax.experimental import pallas as pl
from jax.experimental.pallas import tpu as pltpu
from jax.sharding import Mesh
from jax.sharding import PartitionSpec as P

GROUP = 128
BAND = 16
ROWS = 1024
HALF = 512
QUARTER = 256

momentum_decay = 0.9
step_size = 0.05
replicas = 16

bf16 = jnp.bfloat16
f32 = jnp.float32
HIGHEST = lax.Precision.HIGHEST

SWAP2 = [(0, 1), (1, 0)]
UP4 = [(i, (i + 1) % 4) for i in range(4)]
DOWN4 = [(i, (i + 3) % 4) for i in range(4)]
ACROSS4 = [(i, (i + 2) % 4) for i in range(4)]
EVEN4 = [(0, 1), (1, 0), (2, 3), (3, 2)]
ODD4 = [(1, 2), (2, 1), (3, 0), (0, 3)]
XOR2 = [(i, i ^ 2) for i in range(4)]
CROSS8 = [(i, i ^ 5) for i in range(8)]


def cosine_rows():
    freq = np.arange(BAND, dtype=np.float64)[:, None]
    place = np.arange(GROUP, dtype=np.float64)[None, :]
    factor = np.where(freq == 0.0, np.sqrt(1.0 / GROUP), np.sqrt(2.0 / GROUP))
    return factor * np.cos(np.pi * (2.0 * place + 1.0) * freq / (2.0 * GROUP))


def column_of(dx, gz, core):
    bx = lax.rem(lax.axis_index("x") + dx, 4)
    zh = lax.axis_index("zh")
    bz = zh if gz == 0 else 1 - zh
    return bx * 4 + bz * 2 + core


def slot_of(dx, gz):
    bx = lax.rem(lax.axis_index("x") + dx, 4)
    zh = lax.axis_index("zh")
    return bx * 2 + (zh if gz == 0 else 1 - zh)


def lanes(index):
    return pl.ds(pl.multiple_of(index * GROUP, GROUP), GROUP)


def split_kernel(g_ref, sent_ref, own_ref):
    core = lax.axis_index("core")
    for gz in range(2):
        for dx in range(4):
            k = gz * 4 + dx
            sent_ref[k] = g_ref[:, lanes(column_of(dx, gz, 1 - core))]
            own_ref[k] = g_ref[:, lanes(column_of(dx, gz, core))]


def split_blocks(g):
    blocks = jax.ShapeDtypeStruct((8, ROWS, GROUP), bf16)
    return pl.pallas_call(
        split_kernel,
        out_shape=[blocks, blocks],
        in_specs=[pl.BlockSpec(memory_space=pltpu.VMEM)],
        out_specs=[pl.BlockSpec(memory_space=pltpu.VMEM)] * 2,
        compiler_params=pltpu.CompilerParams(vmem_limit_bytes=12 * 2**20),
    )(g)


def pair_sum_kernel(
    own_ref, other_ref, mom_ref, table_ref, rows_ref, up_ref, down_ref, keep_up_ref, keep_down_ref,
    mine_ref, band_ref, acc_ref,
):
    lane_slot = lax.broadcasted_iota(jnp.int32, (GROUP, GROUP), 1) // BAND
    table = table_ref[...]
    zero = jnp.zeros_like(table)
    for gz in range(2):
        for dx in range(4):
            k = gz * 4 + dx
            s = (own_ref[k].astype(f32) + other_ref[k].astype(f32)).astype(bf16)
            if dx == 0:
                mine_ref[gz] = s
            elif dx == 1:
                keep_up_ref[gz] = s[:HALF]
                up_ref[gz * 2 + 1] = s[HALF:]
            elif dx == 2:
                up_ref[gz * 2] = s[:HALF]
                down_ref[gz * 2] = s[HALF:]
            else:
                down_ref[gz * 2 + 1] = s[:HALF]
                keep_down_ref[gz] = s[HALF:]
            placed = jnp.where(lane_slot == slot_of(dx, gz), table, zero)
            part = jnp.dot(s, placed.astype(bf16), preferred_element_type=f32)
            if k == 0:
                acc_ref[...] = part + jnp.dot(
                    momentum_decay * mom_ref[...], placed, preferred_element_type=f32
                )
            else:
                acc_ref[...] += part
    for a in range(ROWS // GROUP):
        band_ref[a * BAND : (a + 1) * BAND, :] = jnp.dot(
            rows_ref[...],
            acc_ref[a * GROUP : (a + 1) * GROUP, :],
            precision=HIGHEST,
            preferred_element_type=f32,
        )


def pair_sum(*args):
    shapes = [(5, HALF, GROUP)] * 2 + [(2, HALF, GROUP)] * 2 + [(2, ROWS, GROUP)]
    shapes = [jax.ShapeDtypeStruct(shape, bf16) for shape in shapes]
    shapes.append(jax.ShapeDtypeStruct((ROWS // GROUP * BAND, GROUP), f32))
    vmem = pl.BlockSpec(memory_space=pltpu.VMEM)
    return pl.pallas_call(
        pair_sum_kernel,
        out_shape=shapes,
        in_specs=[vmem] * 5,
        out_specs=[vmem] * 6,
        scratch_shapes=[pltpu.VMEM((ROWS, GROUP), f32)],
        compiler_params=pltpu.CompilerParams(vmem_limit_bytes=16 * 2**20),
    )(*args)


def small_call(kernel, shapes, *args, cost=None):
    vmem = pl.BlockSpec(memory_space=pltpu.VMEM)
    return pl.pallas_call(
        kernel,
        out_shape=shapes,
        in_specs=[vmem] * len(args),
        out_specs=jax.tree.map(lambda _: vmem, shapes),
        cost_estimate=cost,
        compiler_params=pltpu.CompilerParams(vmem_limit_bytes=8 * 2**20),
    )(*args)


def join_kernel(first_ref, second_ref, out_ref):
    half = first_ref.shape[0]
    out_ref[:half] = first_ref[...]
    out_ref[half:] = second_ref[...]


def joined(first, second):
    shape = (2 * first.shape[0], *first.shape[1:])
    return small_call(join_kernel, jax.ShapeDtypeStruct(shape, first.dtype), first, second)


def cast_kernel(master_ref, out_ref):
    y = lax.axis_index("y")
    out_ref[...] = master_ref[pl.ds(pl.multiple_of(y * QUARTER, QUARTER), QUARTER), :].astype(bf16)


def enclose_kernel(w0_ref, wz_ref, up_in_ref, down_in_ref, up_ref, down_ref):
    del up_in_ref, down_in_ref
    for ref in (up_ref, down_ref):
        ref[4, :QUARTER] = w0_ref[...]
        ref[4, QUARTER:] = wz_ref[...]


def enclosed(w0, wz, up, down):
    vmem = pl.BlockSpec(memory_space=pltpu.VMEM)
    return pl.pallas_call(
        enclose_kernel,
        out_shape=[jax.ShapeDtypeStruct(up.shape, bf16)] * 2,
        in_specs=[vmem] * 4,
        out_specs=[vmem] * 2,
        input_output_aliases={2: 0, 3: 1},
        compiler_params=pltpu.CompilerParams(vmem_limit_bytes=8 * 2**20),
    )(w0, wz, up, down)


def pass_on_kernel(keep_up_ref, keep_down_ref, left_ref, right_ref, up_ref, down_ref):
    for gz in range(2):
        r = slice(gz * HALF, (gz + 1) * HALF)
        up_ref[r] = (keep_up_ref[gz].astype(f32) + left_ref[gz * 2].astype(f32)).astype(bf16)
        down_ref[r] = (keep_down_ref[gz].astype(f32) + right_ref[gz * 2].astype(f32)).astype(bf16)
    up_ref[2 * HALF :] = left_ref[4, :QUARTER]
    down_ref[2 * HALF :] = right_ref[4, QUARTER:]


def collect_kernel(w0_ref, wz_ref, left_ref, right_ref, last_left_ref, last_right_ref, out_ref):
    out_ref[0] = w0_ref[...]
    out_ref[1] = left_ref[4, :QUARTER]
    out_ref[2] = right_ref[4, :QUARTER]
    out_ref[3] = last_left_ref[2 * HALF :]
    out_ref[4] = wz_ref[...]
    out_ref[5] = left_ref[4, QUARTER:]
    out_ref[6] = right_ref[4, QUARTER:]
    out_ref[7] = last_right_ref[2 * HALF :]


def half_kernel(below_ref, above_ref, low_ref, high_ref):
    low_ref[...] = below_ref[:4]
    high_ref[...] = above_ref[4:]


def pack_kernel(*refs):
    at = 0
    for ref in refs[:-1]:
        refs[-1][at : at + ref.shape[0]] = ref[...]
        at += ref.shape[0]


def packed(*parts):
    blocks = sum(part.shape[0] for part in parts)
    return small_call(pack_kernel, jax.ShapeDtypeStruct((blocks, QUARTER, GROUP), bf16), *parts)


def x_total(mine_ref, left_ref, right_ref, last_left_ref, last_right_ref, gz, a):
    r = slice(a * GROUP, (a + 1) * GROUP)
    h = slice(a % 4 * GROUP, (a % 4 + 1) * GROUP)
    p = slice(gz * HALF + a % 4 * GROUP, gz * HALF + (a % 4 + 1) * GROUP)
    direct, passed = (right_ref, last_left_ref) if a < 4 else (left_ref, last_right_ref)
    total = mine_ref[gz, r].astype(f32) + direct[gz * 2 + 1, h].astype(f32)
    return total + passed[p].astype(f32)


def z_send_kernel(*refs):
    for a in range(ROWS // GROUP):
        refs[5][a * GROUP : (a + 1) * GROUP] = x_total(*refs[:5], 1, a).astype(bf16)


def remaining_kernel(*refs):
    z_ref, mom_ref, q_ref, out_ref = refs[5:]
    q = q_ref[...]
    for a in range(ROWS // GROUP):
        r = slice(a * GROUP, (a + 1) * GROUP)
        summed = x_total(*refs[:5], 0, a) + z_ref[r].astype(f32)
        moment = momentum_decay * mom_ref[r] + summed
        low = jnp.dot(moment, q, precision=HIGHEST, preferred_element_type=f32)
        low = jnp.dot(q, low, precision=HIGHEST, preferred_element_type=f32)
        out_ref[r] = moment - low


def weights_kernel(*refs):
    packs, (band_ref, band_other_ref, master_ref, cols_ref, table_ref) = refs[:4], refs[4:9]
    master_out, full_out, spread_ref, page_ref, sem = refs[9:]
    x, y, zh, core = (lax.axis_index(name) for name in ("x", "y", "zh", "core"))

    row_slot = lax.broadcasted_iota(jnp.int32, (GROUP, GROUP), 0) // BAND
    table = table_ref[...]
    zero = jnp.zeros_like(table)
    columns = []
    wide = []
    for gz, dx in [(gz, dx) for gz in range(2) for dx in (0, 3, 1, 2)]:
        bx, bz = lax.rem(x + dx, 4), (zh if gz == 0 else 1 - zh)
        columns.append(bx * 4 + bz * 2)
        wide.append(jnp.where(row_slot == bx * 2 + bz, table, zero).astype(bf16))
    wide = jnp.concatenate(wide, axis=1)

    coeffs = jnp.concatenate([band_ref[...], band_other_ref[...]], axis=1)
    spread_ref[...] = jnp.dot(
        cols_ref[...], coeffs.astype(bf16), preferred_element_type=f32
    ).astype(bf16)

    copies = []
    for step, dy in enumerate((0, 3, 1, 2)):
        quarter = lax.rem(y + dy, 4)
        rows = pl.ds(pl.multiple_of(quarter * QUARTER, QUARTER), QUARTER)
        for who in range(2):
            side = core if who == 0 else 1 - core
            update = jnp.dot(
                spread_ref[rows, who * GROUP : (who + 1) * GROUP],
                wide,
                preferred_element_type=f32,
            )
            for k in range(8):
                part = update[:, k * GROUP : (k + 1) * GROUP]
                prior = packs[2 + who][k] if step == 3 else packs[who][step * 8 + k]
                new = prior.astype(f32) + part
                page_ref[step, :, lanes(columns[k] + side)] = new.astype(bf16)
        copy = pltpu.make_async_copy(page_ref.at[step], full_out.at[rows, :], sem.at[step])
        copy.start()
        copies.append(copy)
    master_out[...] = master_ref[...] + jnp.dot(
        spread_ref[:, :GROUP], wide[:, :GROUP], preferred_element_type=f32
    )
    for copy in copies:
        copy.wait()


def weights_of(packs, bands, master, cols, table):
    vmem = pl.BlockSpec(memory_space=pltpu.VMEM)
    return pl.pallas_call(
        weights_kernel,
        out_shape=[
            jax.ShapeDtypeStruct((ROWS, GROUP), f32),
            jax.ShapeDtypeStruct((ROWS, 16 * GROUP), bf16),
        ],
        in_specs=[vmem] * 9,
        out_specs=[vmem, pl.BlockSpec(memory_space=pl.ANY)],
        scratch_shapes=[
            pltpu.VMEM((ROWS, 2 * GROUP), bf16),
            pltpu.VMEM((4, QUARTER, 16 * GROUP), bf16),
            pltpu.SemaphoreType.DMA((4,)),
        ],
        compiler_params=pltpu.CompilerParams(vmem_limit_bytes=20 * 2**20),
    )(*packs, *bands, master, cols, table)


def send(array, axis, perm):
    return lax.ppermute(array, axis, perm)


together = lax.optimization_barrier


def local(gradients, momentum, master_weights):
    table = cosine_rows()
    mom = momentum[0]
    half = (ROWS, GROUP)
    z = ("zl", "zh")

    sent, own = split_blocks(gradients[0, 0])
    other = send(sent, "core", SWAP2)
    w0 = small_call(cast_kernel, jax.ShapeDtypeStruct((QUARTER, GROUP), bf16), master_weights)
    wz = send(w0, z, CROSS8)
    up, down, keep_up, keep_down, mine, band = pair_sum(
        own,
        other,
        mom,
        jnp.asarray(np.tile(table.T, (1, 8)), f32),
        jnp.asarray(table, f32),
    )

    got = send(band, "zl", EVEN4)
    up, down = enclosed(w0, wz, up, down)
    left = send(up, "x", UP4)
    right = send(down, "x", DOWN4)

    band = band + got
    got = send(band, "y", EVEN4)

    band = band + got
    got = send(band, "y", ODD4)

    band, left, right = together((band + got, left, right))
    got = send(band, "zl", XOR2)
    passed = jax.ShapeDtypeStruct((2 * HALF + QUARTER, GROUP), bf16)
    up, down = small_call(pass_on_kernel, [passed] * 2, keep_up, keep_down, left, right)
    last_left = send(up, "x", UP4)
    last_right = send(down, "x", DOWN4)

    band, last_left, last_right = together((band + got, last_left, last_right))
    got = send(band, z, CROSS8)
    parts = (mine, left, right, last_left, last_right)
    eighth = small_call(
        collect_kernel, jax.ShapeDtypeStruct((8, QUARTER, GROUP), bf16), w0, wz, *parts[1:]
    )
    below = send(eighth, "y", UP4)
    above = send(eighth, "y", DOWN4)
    z_send = small_call(z_send_kernel, jax.ShapeDtypeStruct(half, bf16), *parts)

    band, z_send = together((band + got, z_send))
    got = send(band, "x", EVEN4)
    from_z = send(z_send, "zh", SWAP2)

    band, eighth, below, above = together((band + got, eighth, below, above))
    got = send(band, "x", ODD4)
    four = jax.ShapeDtypeStruct((4, QUARTER, GROUP), bf16)
    up, down = small_call(half_kernel, [four] * 2, below, above)
    low = send(up, "y", UP4)
    high = send(down, "y", DOWN4)
    new_momentum = small_call(
        remaining_kernel,
        jax.ShapeDtypeStruct(half, f32),
        *parts,
        from_z,
        mom,
        jnp.asarray(table.T @ table, f32),
        cost=pl.CostEstimate(flops=8000000000, bytes_accessed=2000000, transcendentals=0),
    )

    band, low, high, new_momentum = together(
        ((band + got) * (-step_size / replicas), low, high, new_momentum)
    )
    band_other = send(band, "core", SWAP2)
    early = packed(eighth, below, above)
    early_other = send(early, "core", SWAP2)
    late = packed(low, high)
    late_other = send(late, "core", SWAP2)
    new_master, weights_full = weights_of(
        (early, early_other, late, late_other),
        (band, band_other),
        master_weights,
        jnp.asarray(np.kron(np.eye(8), table.T), bf16),
        jnp.asarray(np.tile(table, (8, 1)), f32),
    )
    return (new_momentum[None], new_master, weights_full)


def solution(mesh):
    fine = Mesh(mesh.devices.reshape(4, 4, 4, 2, 2), ("y", "zl", "x", "zh", "core"))
    rep, fsdp = ("y", "zl"), ("x", "zh", "core")
    return jax.shard_map(
        local,
        mesh=fine,
        in_specs=(P(rep, fsdp, None, None), P(rep, None, fsdp), P(None, fsdp)),
        out_specs=(P(rep, None, fsdp), P(None, fsdp), P()),
        check_vma=False,
    )
```

```python
import functools

import jax
import jax.numpy as jnp
import numpy as np
from jax import lax
from jax.experimental import pallas as pl
from jax.experimental.pallas import tpu as pltpu
from jax.sharding import Mesh
from jax.sharding import PartitionSpec as P

GROUP = 128
BAND = 16
ROWS = 1024
HALF = 512
QUARTER = 256

momentum_decay = 0.9
step_size = 0.05
replicas = 16

bf16 = jnp.bfloat16
f32 = jnp.float32
HIGHEST = lax.Precision.HIGHEST

SWAP2 = [(0, 1), (1, 0)]
UP4 = [(i, (i + 1) % 4) for i in range(4)]
DOWN4 = [(i, (i + 3) % 4) for i in range(4)]
ACROSS4 = [(i, (i + 2) % 4) for i in range(4)]
EVEN4 = [(0, 1), (1, 0), (2, 3), (3, 2)]
ODD4 = [(1, 2), (2, 1), (3, 0), (0, 3)]
XOR2 = [(i, i ^ 2) for i in range(4)]
CROSS8 = [(i, i ^ 5) for i in range(8)]


def cosine_rows():
    freq = np.arange(BAND, dtype=np.float64)[:, None]
    place = np.arange(GROUP, dtype=np.float64)[None, :]
    factor = np.where(freq == 0.0, np.sqrt(1.0 / GROUP), np.sqrt(2.0 / GROUP))
    return factor * np.cos(np.pi * (2.0 * place + 1.0) * freq / (2.0 * GROUP))


def column_of(dx, gz, core):
    bx = lax.rem(lax.axis_index("x") + dx, 4)
    zh = lax.axis_index("zh")
    bz = zh if gz == 0 else 1 - zh
    return bx * 4 + bz * 2 + core


def slot_of(dx, gz):
    bx = lax.rem(lax.axis_index("x") + dx, 4)
    zh = lax.axis_index("zh")
    return bx * 2 + (zh if gz == 0 else 1 - zh)


def lanes(index):
    return pl.ds(pl.multiple_of(index * GROUP, GROUP), GROUP)


def split_kernel(g_ref, sent_ref, own_ref):
    core = lax.axis_index("core")
    for gz in range(2):
        for dx in range(4):
            k = gz * 4 + dx
            sent_ref[k] = g_ref[:, lanes(column_of(dx, gz, 1 - core))]
            own_ref[k] = g_ref[:, lanes(column_of(dx, gz, core))]


def split_blocks(g):
    blocks = jax.ShapeDtypeStruct((8, ROWS, GROUP), bf16)
    return pl.pallas_call(
        split_kernel,
        out_shape=[blocks, blocks],
        in_specs=[pl.BlockSpec(memory_space=pltpu.VMEM)],
        out_specs=[pl.BlockSpec(memory_space=pltpu.VMEM)] * 2,
        compiler_params=pltpu.CompilerParams(vmem_limit_bytes=12 * 2**20),
    )(g)


def pair_sum_kernel(
    own_ref, other_ref, mom_ref, table_ref, rows_ref, up_ref, down_ref, keep_up_ref, keep_down_ref,
    mine_ref, band_ref, acc_ref,
):
    lane_slot = lax.broadcasted_iota(jnp.int32, (GROUP, GROUP), 1) // BAND
    table = table_ref[...]
    zero = jnp.zeros_like(table)
    for gz in range(2):
        for dx in range(4):
            k = gz * 4 + dx
            s = (own_ref[k].astype(f32) + other_ref[k].astype(f32)).astype(bf16)
            if dx == 0:
                mine_ref[gz] = s
            elif dx == 1:
                keep_up_ref[gz] = s[:HALF]
                up_ref[gz * 2 + 1] = s[HALF:]
            elif dx == 2:
                up_ref[gz * 2] = s[:HALF]
                down_ref[gz * 2] = s[HALF:]
            else:
                down_ref[gz * 2 + 1] = s[:HALF]
                keep_down_ref[gz] = s[HALF:]
            placed = jnp.where(lane_slot == slot_of(dx, gz), table, zero)
            part = jnp.dot(s, placed.astype(bf16), preferred_element_type=f32)
            if k == 0:
                acc_ref[...] = part + jnp.dot(
                    momentum_decay * mom_ref[...], placed, preferred_element_type=f32
                )
            else:
                acc_ref[...] += part
    for a in range(ROWS // GROUP):
        band_ref[a * BAND : (a + 1) * BAND, :] = jnp.dot(
            rows_ref[...],
            acc_ref[a * GROUP : (a + 1) * GROUP, :],
            precision=HIGHEST,
            preferred_element_type=f32,
        )


def pair_sum(*args):
    shapes = [(5, HALF, GROUP)] * 2 + [(2, HALF, GROUP)] * 2 + [(2, ROWS, GROUP)]
    shapes = [jax.ShapeDtypeStruct(shape, bf16) for shape in shapes]
    shapes.append(jax.ShapeDtypeStruct((ROWS // GROUP * BAND, GROUP), f32))
    vmem = pl.BlockSpec(memory_space=pltpu.VMEM)
    return pl.pallas_call(
        pair_sum_kernel,
        out_shape=shapes,
        in_specs=[vmem] * 5,
        out_specs=[vmem] * 6,
        scratch_shapes=[pltpu.VMEM((ROWS, GROUP), f32)],
        compiler_params=pltpu.CompilerParams(vmem_limit_bytes=16 * 2**20),
    )(*args)


def small_call(kernel, shapes, *args, cost=None):
    vmem = pl.BlockSpec(memory_space=pltpu.VMEM)
    return pl.pallas_call(
        kernel,
        out_shape=shapes,
        in_specs=[vmem] * len(args),
        out_specs=jax.tree.map(lambda _: vmem, shapes),
        cost_estimate=cost,
        compiler_params=pltpu.CompilerParams(vmem_limit_bytes=8 * 2**20),
    )(*args)


def join_kernel(first_ref, second_ref, out_ref):
    half = first_ref.shape[0]
    out_ref[:half] = first_ref[...]
    out_ref[half:] = second_ref[...]


def joined(first, second):
    shape = (2 * first.shape[0], *first.shape[1:])
    return small_call(join_kernel, jax.ShapeDtypeStruct(shape, first.dtype), first, second)


def cast_kernel(master_ref, out_ref):
    y = lax.axis_index("y")
    out_ref[...] = master_ref[pl.ds(pl.multiple_of(y * QUARTER, QUARTER), QUARTER), :].astype(bf16)


def enclose_kernel(w0_ref, wz_ref, up_in_ref, down_in_ref, up_ref, down_ref):
    del up_in_ref, down_in_ref
    for ref in (up_ref, down_ref):
        ref[4, :QUARTER] = w0_ref[...]
        ref[4, QUARTER:] = wz_ref[...]


def enclosed(w0, wz, up, down):
    vmem = pl.BlockSpec(memory_space=pltpu.VMEM)
    return pl.pallas_call(
        enclose_kernel,
        out_shape=[jax.ShapeDtypeStruct(up.shape, bf16)] * 2,
        in_specs=[vmem] * 4,
        out_specs=[vmem] * 2,
        input_output_aliases={2: 0, 3: 1},
        compiler_params=pltpu.CompilerParams(vmem_limit_bytes=8 * 2**20),
    )(w0, wz, up, down)


def pass_on_kernel(keep_up_ref, keep_down_ref, left_ref, right_ref, up_ref, down_ref):
    for gz in range(2):
        r = slice(gz * HALF, (gz + 1) * HALF)
        up_ref[r] = (keep_up_ref[gz].astype(f32) + left_ref[gz * 2].astype(f32)).astype(bf16)
        down_ref[r] = (keep_down_ref[gz].astype(f32) + right_ref[gz * 2].astype(f32)).astype(bf16)
    up_ref[2 * HALF :] = left_ref[4, :QUARTER]
    down_ref[2 * HALF :] = right_ref[4, QUARTER:]


def collect_kernel(w0_ref, wz_ref, left_ref, right_ref, last_left_ref, last_right_ref, out_ref):
    out_ref[0] = w0_ref[...]
    out_ref[1] = left_ref[4, :QUARTER]
    out_ref[2] = right_ref[4, :QUARTER]
    out_ref[3] = last_left_ref[2 * HALF :]
    out_ref[4] = wz_ref[...]
    out_ref[5] = left_ref[4, QUARTER:]
    out_ref[6] = right_ref[4, QUARTER:]
    out_ref[7] = last_right_ref[2 * HALF :]


def half_kernel(below_ref, above_ref, low_ref, high_ref):
    low_ref[...] = below_ref[:4]
    high_ref[...] = above_ref[4:]


def pack_kernel(*refs):
    at = 0
    for ref in refs[:-1]:
        refs[-1][at : at + ref.shape[0]] = ref[...]
        at += ref.shape[0]


def packed(*parts):
    blocks = sum(part.shape[0] for part in parts)
    return small_call(pack_kernel, jax.ShapeDtypeStruct((blocks, QUARTER, GROUP), bf16), *parts)


def x_total(mine_ref, left_ref, right_ref, last_left_ref, last_right_ref, gz, a):
    r = slice(a * GROUP, (a + 1) * GROUP)
    h = slice(a % 4 * GROUP, (a % 4 + 1) * GROUP)
    p = slice(gz * HALF + a % 4 * GROUP, gz * HALF + (a % 4 + 1) * GROUP)
    direct, passed = (right_ref, last_left_ref) if a < 4 else (left_ref, last_right_ref)
    total = mine_ref[gz, r].astype(f32) + direct[gz * 2 + 1, h].astype(f32)
    return total + passed[p].astype(f32)


def z_send_kernel(*refs):
    for a in range(ROWS // GROUP):
        refs[5][a * GROUP : (a + 1) * GROUP] = x_total(*refs[:5], 1, a).astype(bf16)


def remaining_kernel(*refs):
    z_ref, mom_ref, q_ref, out_ref = refs[5:]
    q = q_ref[...]
    for a in range(ROWS // GROUP):
        r = slice(a * GROUP, (a + 1) * GROUP)
        summed = x_total(*refs[:5], 0, a) + z_ref[r].astype(f32)
        moment = momentum_decay * mom_ref[r] + summed
        low = jnp.dot(moment, q, precision=HIGHEST, preferred_element_type=f32)
        low = jnp.dot(q, low, precision=HIGHEST, preferred_element_type=f32)
        out_ref[r] = moment - low


def weights_kernel(*refs):
    packs, (band_ref, band_other_ref, master_ref, cols_ref, table_ref) = refs[:4], refs[4:9]
    master_out, full_out, spread_ref, page_ref, sem = refs[9:]
    x, y, zh, core = (lax.axis_index(name) for name in ("x", "y", "zh", "core"))

    row_slot = lax.broadcasted_iota(jnp.int32, (GROUP, GROUP), 0) // BAND
    table = table_ref[...]
    zero = jnp.zeros_like(table)
    columns = []
    wide = []
    for gz, dx in [(gz, dx) for gz in range(2) for dx in (0, 3, 1, 2)]:
        bx, bz = lax.rem(x + dx, 4), (zh if gz == 0 else 1 - zh)
        columns.append(bx * 4 + bz * 2)
        wide.append(jnp.where(row_slot == bx * 2 + bz, table, zero).astype(bf16))
    wide = jnp.concatenate(wide, axis=1)

    coeffs = jnp.concatenate([band_ref[...], band_other_ref[...]], axis=1)
    spread_ref[...] = jnp.dot(
        cols_ref[...], coeffs, preferred_element_type=f32
    ).astype(bf16)

    copies = []
    for step, dy in enumerate((0, 3, 1, 2)):
        quarter = lax.rem(y + dy, 4)
        rows = pl.ds(pl.multiple_of(quarter * QUARTER, QUARTER), QUARTER)
        for who in range(2):
            side = core if who == 0 else 1 - core
            update = jnp.dot(
                spread_ref[rows, who * GROUP : (who + 1) * GROUP],
                wide,
                preferred_element_type=f32,
            )
            for k in range(8):
                part = update[:, k * GROUP : (k + 1) * GROUP]
                prior = packs[2 + who][k] if step == 3 else packs[who][step * 8 + k]
                new = prior.astype(f32) + part
                page_ref[step, :, lanes(columns[k] + side)] = new.astype(bf16)
        copy = pltpu.make_async_copy(page_ref.at[step], full_out.at[rows, :], sem.at[step])
        copy.start()
        copies.append(copy)
    master_out[...] = master_ref[...] + jnp.dot(
        spread_ref[:, :GROUP], wide[:, :GROUP], preferred_element_type=f32
    )
    for copy in copies:
        copy.wait()


def weights_of(packs, bands, master, cols, table):
    vmem = pl.BlockSpec(memory_space=pltpu.VMEM)
    return pl.pallas_call(
        weights_kernel,
        out_shape=[
            jax.ShapeDtypeStruct((ROWS, GROUP), f32),
            jax.ShapeDtypeStruct((ROWS, 16 * GROUP), bf16),
        ],
        in_specs=[vmem] * 9,
        out_specs=[vmem, pl.BlockSpec(memory_space=pl.ANY)],
        scratch_shapes=[
            pltpu.VMEM((ROWS, 2 * GROUP), bf16),
            pltpu.VMEM((4, QUARTER, 16 * GROUP), bf16),
            pltpu.SemaphoreType.DMA((4,)),
        ],
        compiler_params=pltpu.CompilerParams(vmem_limit_bytes=20 * 2**20),
    )(*packs, *bands, master, cols, table)


def send(array, axis, perm):
    return lax.ppermute(array, axis, perm)


together = lax.optimization_barrier


def both(own, got):
    return own.astype(f32) + got.astype(f32)


def local(gradients, momentum, master_weights):
    table = cosine_rows()
    mom = momentum[0]
    half = (ROWS, GROUP)
    z = ("zl", "zh")

    sent, own = split_blocks(gradients[0, 0])
    other = send(sent, "core", SWAP2)
    w0 = small_call(cast_kernel, jax.ShapeDtypeStruct((QUARTER, GROUP), bf16), master_weights)
    wz = send(w0, z, CROSS8)
    up, down, keep_up, keep_down, mine, band = pair_sum(
        own,
        other,
        mom,
        jnp.asarray(np.tile(table.T, (1, 8)), f32),
        jnp.asarray(table, f32),
    )

    band = band.astype(bf16)
    got = send(band, "zl", EVEN4)
    up, down = enclosed(w0, wz, up, down)
    left = send(up, "x", UP4)
    right = send(down, "x", DOWN4)

    band = both(band, got)
    band = band.astype(bf16)
    got = send(band, "y", EVEN4)

    band = both(band, got)
    band = band.astype(bf16)
    got = send(band, "y", ODD4)

    band, left, right = together((both(band, got), left, right))
    band = band.astype(bf16)
    got = send(band, "zl", XOR2)
    passed = jax.ShapeDtypeStruct((2 * HALF + QUARTER, GROUP), bf16)
    up, down = small_call(pass_on_kernel, [passed] * 2, keep_up, keep_down, left, right)
    last_left = send(up, "x", UP4)
    last_right = send(down, "x", DOWN4)

    band, last_left, last_right = together((both(band, got), last_left, last_right))
    band = band.astype(bf16)
    got = send(band, z, CROSS8)
    parts = (mine, left, right, last_left, last_right)
    eighth = small_call(
        collect_kernel, jax.ShapeDtypeStruct((8, QUARTER, GROUP), bf16), w0, wz, *parts[1:]
    )
    below = send(eighth, "y", UP4)
    above = send(eighth, "y", DOWN4)
    z_send = small_call(z_send_kernel, jax.ShapeDtypeStruct(half, bf16), *parts)

    band, z_send = together((both(band, got), z_send))
    band = band.astype(bf16)
    got = send(band, "x", EVEN4)
    from_z = send(z_send, "zh", SWAP2)

    band, eighth, below, above = together((both(band, got), eighth, below, above))
    band = band.astype(bf16)
    got = send(band, "x", ODD4)
    four = jax.ShapeDtypeStruct((4, QUARTER, GROUP), bf16)
    up, down = small_call(half_kernel, [four] * 2, below, above)
    low = send(up, "y", UP4)
    high = send(down, "y", DOWN4)
    new_momentum = small_call(
        remaining_kernel,
        jax.ShapeDtypeStruct(half, f32),
        *parts,
        from_z,
        mom,
        jnp.asarray(table.T @ table, f32),
        cost=pl.CostEstimate(flops=8000000000, bytes_accessed=2000000, transcendentals=0),
    )

    band, low, high, new_momentum = together(
        ((both(band, got)) * (-step_size / replicas), low, high, new_momentum)
    )
    band = band.astype(bf16)
    band_other = send(band, "core", SWAP2)
    early = packed(eighth, below, above)
    early_other = send(early, "core", SWAP2)
    late = packed(low, high)
    late_other = send(late, "core", SWAP2)
    new_master, weights_full = weights_of(
        (early, early_other, late, late_other),
        (band, band_other),
        master_weights,
        jnp.asarray(np.kron(np.eye(8), table.T), bf16),
        jnp.asarray(np.tile(table, (8, 1)), f32),
    )
    return (new_momentum[None], new_master, weights_full)


def solution(mesh):
    fine = Mesh(mesh.devices.reshape(4, 4, 4, 2, 2), ("y", "zl", "x", "zh", "core"))
    rep, fsdp = ("y", "zl"), ("x", "zh", "core")
    return jax.shard_map(
        local,
        mesh=fine,
        in_specs=(P(rep, fsdp, None, None), P(rep, None, fsdp), P(None, fsdp)),
        out_specs=(P(rep, None, fsdp), P(None, fsdp), P()),
        check_vma=False,
    )
```

```python
import functools

import jax
import jax.numpy as jnp
import numpy as np
from jax import lax
from jax.experimental import pallas as pl
from jax.experimental.pallas import tpu as pltpu
from jax.sharding import Mesh
from jax.sharding import PartitionSpec as P

GROUP = 128
BAND = 16
ROWS = 1024
HALF = 512
QUARTER = 256

momentum_decay = 0.9
step_size = 0.05
replicas = 16

bf16 = jnp.bfloat16
f32 = jnp.float32
HIGHEST = lax.Precision.HIGHEST

SWAP2 = [(0, 1), (1, 0)]
UP4 = [(i, (i + 1) % 4) for i in range(4)]
DOWN4 = [(i, (i + 3) % 4) for i in range(4)]
ACROSS4 = [(i, (i + 2) % 4) for i in range(4)]
EVEN4 = [(0, 1), (1, 0), (2, 3), (3, 2)]
ODD4 = [(1, 2), (2, 1), (3, 0), (0, 3)]
XOR2 = [(i, i ^ 2) for i in range(4)]
CROSS8 = [(i, i ^ 5) for i in range(8)]


def cosine_rows():
    freq = np.arange(BAND, dtype=np.float64)[:, None]
    place = np.arange(GROUP, dtype=np.float64)[None, :]
    factor = np.where(freq == 0.0, np.sqrt(1.0 / GROUP), np.sqrt(2.0 / GROUP))
    return factor * np.cos(np.pi * (2.0 * place + 1.0) * freq / (2.0 * GROUP))


def column_of(dx, gz, core):
    bx = lax.rem(lax.axis_index("x") + dx, 4)
    zh = lax.axis_index("zh")
    bz = zh if gz == 0 else 1 - zh
    return bx * 4 + bz * 2 + core


def slot_of(dx, gz):
    bx = lax.rem(lax.axis_index("x") + dx, 4)
    zh = lax.axis_index("zh")
    return bx * 2 + (zh if gz == 0 else 1 - zh)


def lanes(index):
    return pl.ds(pl.multiple_of(index * GROUP, GROUP), GROUP)


def split_kernel(g_ref, sent_ref, own_ref):
    core = lax.axis_index("core")
    for gz in range(2):
        for dx in range(4):
            k = gz * 4 + dx
            sent_ref[k] = g_ref[:, lanes(column_of(dx, gz, 1 - core))]
            own_ref[k] = g_ref[:, lanes(column_of(dx, gz, core))]


def split_blocks(g):
    blocks = jax.ShapeDtypeStruct((8, ROWS, GROUP), bf16)
    return pl.pallas_call(
        split_kernel,
        out_shape=[blocks, blocks],
        in_specs=[pl.BlockSpec(memory_space=pltpu.VMEM)],
        out_specs=[pl.BlockSpec(memory_space=pltpu.VMEM)] * 2,
        compiler_params=pltpu.CompilerParams(vmem_limit_bytes=12 * 2**20),
    )(g)


def pair_sum_kernel(
    own_ref, other_ref, mom_ref, table_ref, rows_ref, up_ref, down_ref, keep_up_ref, keep_down_ref,
    mine_ref, band_ref, acc_ref,
):
    lane_slot = lax.broadcasted_iota(jnp.int32, (GROUP, GROUP), 1) // BAND
    table = table_ref[...]
    zero = jnp.zeros_like(table)
    for gz in range(2):
        for dx in range(4):
            k = gz * 4 + dx
            s = (own_ref[k].astype(f32) + other_ref[k].astype(f32)).astype(bf16)
            if dx == 0:
                mine_ref[gz] = s
            elif dx == 1:
                keep_up_ref[gz] = s[:HALF]
                up_ref[gz * 2 + 1] = s[HALF:]
            elif dx == 2:
                up_ref[gz * 2] = s[:HALF]
                down_ref[gz * 2] = s[HALF:]
            else:
                down_ref[gz * 2 + 1] = s[:HALF]
                keep_down_ref[gz] = s[HALF:]
            placed = jnp.where(lane_slot == slot_of(dx, gz), table, zero)
            part = jnp.dot(s, placed.astype(bf16), preferred_element_type=f32)
            if k == 0:
                acc_ref[...] = part + jnp.dot(
                    momentum_decay * mom_ref[...], placed, preferred_element_type=f32
                )
            else:
                acc_ref[...] += part
    for a in range(ROWS // GROUP):
        band_ref[a * BAND : (a + 1) * BAND, :] = jnp.dot(
            rows_ref[...],
            acc_ref[a * GROUP : (a + 1) * GROUP, :],
            precision=HIGHEST,
            preferred_element_type=f32,
        )


def pair_sum(*args):
    shapes = [(5, HALF, GROUP)] * 2 + [(2, HALF, GROUP)] * 2 + [(2, ROWS, GROUP)]
    shapes = [jax.ShapeDtypeStruct(shape, bf16) for shape in shapes]
    shapes.append(jax.ShapeDtypeStruct((ROWS // GROUP * BAND, GROUP), f32))
    vmem = pl.BlockSpec(memory_space=pltpu.VMEM)
    return pl.pallas_call(
        pair_sum_kernel,
        out_shape=shapes,
        in_specs=[vmem] * 5,
        out_specs=[vmem] * 6,
        scratch_shapes=[pltpu.VMEM((ROWS, GROUP), f32)],
        compiler_params=pltpu.CompilerParams(vmem_limit_bytes=16 * 2**20),
    )(*args)


def small_call(kernel, shapes, *args, cost=None):
    vmem = pl.BlockSpec(memory_space=pltpu.VMEM)
    return pl.pallas_call(
        kernel,
        out_shape=shapes,
        in_specs=[vmem] * len(args),
        out_specs=jax.tree.map(lambda _: vmem, shapes),
        cost_estimate=cost,
        compiler_params=pltpu.CompilerParams(vmem_limit_bytes=8 * 2**20),
    )(*args)


def join_kernel(first_ref, second_ref, out_ref):
    half = first_ref.shape[0]
    out_ref[:half] = first_ref[...]
    out_ref[half:] = second_ref[...]


def joined(first, second):
    shape = (2 * first.shape[0], *first.shape[1:])
    return small_call(join_kernel, jax.ShapeDtypeStruct(shape, first.dtype), first, second)


def cast_kernel(master_ref, out_ref):
    y = lax.axis_index("y")
    out_ref[...] = master_ref[pl.ds(pl.multiple_of(y * QUARTER, QUARTER), QUARTER), :].astype(bf16)


def enclose_kernel(w0_ref, wz_ref, up_in_ref, down_in_ref, up_ref, down_ref):
    del up_in_ref, down_in_ref
    for ref in (up_ref, down_ref):
        ref[4, :QUARTER] = w0_ref[...]
        ref[4, QUARTER:] = wz_ref[...]


def enclosed(w0, wz, up, down):
    vmem = pl.BlockSpec(memory_space=pltpu.VMEM)
    return pl.pallas_call(
        enclose_kernel,
        out_shape=[jax.ShapeDtypeStruct(up.shape, bf16)] * 2,
        in_specs=[vmem] * 4,
        out_specs=[vmem] * 2,
        input_output_aliases={2: 0, 3: 1},
        compiler_params=pltpu.CompilerParams(vmem_limit_bytes=8 * 2**20),
    )(w0, wz, up, down)


def pass_on_kernel(keep_up_ref, keep_down_ref, left_ref, right_ref, up_ref, down_ref):
    for gz in range(2):
        r = slice(gz * HALF, (gz + 1) * HALF)
        up_ref[r] = (keep_up_ref[gz].astype(f32) + left_ref[gz * 2].astype(f32)).astype(bf16)
        down_ref[r] = (keep_down_ref[gz].astype(f32) + right_ref[gz * 2].astype(f32)).astype(bf16)
    up_ref[2 * HALF :] = left_ref[4, :QUARTER]
    down_ref[2 * HALF :] = right_ref[4, QUARTER:]


def collect_kernel(w0_ref, wz_ref, left_ref, right_ref, last_left_ref, last_right_ref, out_ref):
    out_ref[0] = w0_ref[...]
    out_ref[1] = left_ref[4, :QUARTER]
    out_ref[2] = right_ref[4, :QUARTER]
    out_ref[3] = last_left_ref[2 * HALF :]
    out_ref[4] = wz_ref[...]
    out_ref[5] = left_ref[4, QUARTER:]
    out_ref[6] = right_ref[4, QUARTER:]
    out_ref[7] = last_right_ref[2 * HALF :]


def half_kernel(below_ref, above_ref, low_ref, high_ref):
    low_ref[...] = below_ref[:4]
    high_ref[...] = above_ref[4:]


def pack_kernel(*refs):
    at = 0
    for ref in refs[:-1]:
        refs[-1][at : at + ref.shape[0]] = ref[...]
        at += ref.shape[0]


def packed(*parts):
    blocks = sum(part.shape[0] for part in parts)
    return small_call(pack_kernel, jax.ShapeDtypeStruct((blocks, QUARTER, GROUP), bf16), *parts)


def x_total(mine_ref, left_ref, right_ref, last_left_ref, last_right_ref, gz, a):
    r = slice(a * GROUP, (a + 1) * GROUP)
    h = slice(a % 4 * GROUP, (a % 4 + 1) * GROUP)
    p = slice(gz * HALF + a % 4 * GROUP, gz * HALF + (a % 4 + 1) * GROUP)
    direct, passed = (right_ref, last_left_ref) if a < 4 else (left_ref, last_right_ref)
    total = mine_ref[gz, r].astype(f32) + direct[gz * 2 + 1, h].astype(f32)
    return total + passed[p].astype(f32)


def z_send_kernel(*refs):
    for a in range(ROWS // GROUP):
        refs[5][a * GROUP : (a + 1) * GROUP] = x_total(*refs[:5], 1, a).astype(bf16)


def remaining_kernel(*refs):
    z_ref, mom_ref, q_ref, out_ref = refs[5:]
    q = q_ref[...]
    for a in range(ROWS // GROUP):
        r = slice(a * GROUP, (a + 1) * GROUP)
        summed = x_total(*refs[:5], 0, a) + z_ref[r].astype(f32)
        moment = momentum_decay * mom_ref[r] + summed
        low = jnp.dot(moment, q, precision=HIGHEST, preferred_element_type=f32)
        low = jnp.dot(q, low, precision=HIGHEST, preferred_element_type=f32)
        out_ref[r] = moment - low


def columns_side(table_ref):
    x, zh = lax.axis_index("x"), lax.axis_index("zh")
    row_slot = lax.broadcasted_iota(jnp.int32, (GROUP, GROUP), 0) // BAND
    table = table_ref[...]
    zero = jnp.zeros_like(table)
    columns = []
    wide = []
    for gz in range(2):
        for dx in (0, 3, 1, 2):
            bx, bz = lax.rem(x + dx, 4), (zh if gz == 0 else 1 - zh)
            columns.append(bx * 4 + bz * 2)
            wide.append(jnp.where(row_slot == bx * 2 + bz, table, zero).astype(bf16))
    return jnp.concatenate(wide, axis=1), columns


def update_quarter(dy, packs, at, spread_ref, wide, columns, page_ref, full_out, sem):
    core = lax.axis_index("core")
    quarter = lax.rem(lax.axis_index("y") + dy, 4)
    rows = pl.ds(pl.multiple_of(quarter * QUARTER, QUARTER), QUARTER)
    for who in range(2):
        side = core if who == 0 else 1 - core
        update = jnp.dot(
            spread_ref[rows, who * GROUP : (who + 1) * GROUP], wide, preferred_element_type=f32
        )
        for k, column in enumerate(columns):
            new = packs[who][at + k].astype(f32) + update[:, k * GROUP : (k + 1) * GROUP]
            page_ref[:, lanes(column + side)] = new.astype(bf16)
    copy = pltpu.make_async_copy(page_ref, full_out.at[rows, :], sem)
    copy.start()
    return copy


def first_weights_kernel(
    early_ref, early_other_ref, band_ref, band_other_ref, master_ref, cols_ref, table_ref,
    master_out, full_out, spread_ref, page_ref, sem,
):
    wide, columns = columns_side(table_ref)
    coeffs = jnp.concatenate([band_ref[...], band_other_ref[...]], axis=1)
    spread_ref[...] = jnp.dot(
        cols_ref[...], coeffs, preferred_element_type=f32
    ).astype(bf16)
    packs = (early_ref, early_other_ref)
    copies = [
        update_quarter(
            dy, packs, 8 * step, spread_ref, wide, columns, page_ref.at[step], full_out, sem.at[step]
        )
        for step, dy in enumerate((0, 3, 1))
    ]
    master_out[...] = master_ref[...] + jnp.dot(
        spread_ref[:, :GROUP], wide[:, :GROUP], preferred_element_type=f32
    )
    for copy in copies:
        copy.wait()


def last_weights_kernel(
    late_ref, late_other_ref, spread_ref, table_ref, started_ref, full_out, page_ref, sem
):
    del started_ref
    wide, columns = columns_side(table_ref)
    packs = (late_ref, late_other_ref)
    update_quarter(2, packs, 0, spread_ref, wide, columns, page_ref, full_out, sem).wait()


VMEM = pl.BlockSpec(memory_space=pltpu.VMEM)
ANYWHERE = pl.BlockSpec(memory_space=pl.ANY)
FULL = jax.ShapeDtypeStruct((ROWS, 16 * GROUP), bf16)


def first_weights(early, early_other, band, band_other, master, cols, table):
    return pl.pallas_call(
        first_weights_kernel,
        out_shape=[
            jax.ShapeDtypeStruct((ROWS, GROUP), f32),
            FULL,
            jax.ShapeDtypeStruct((ROWS, 2 * GROUP), bf16),
        ],
        in_specs=[VMEM] * 7,
        out_specs=[VMEM, ANYWHERE, VMEM],
        scratch_shapes=[
            pltpu.VMEM((3, QUARTER, 16 * GROUP), bf16),
            pltpu.SemaphoreType.DMA((3,)),
        ],
        compiler_params=pltpu.CompilerParams(vmem_limit_bytes=20 * 2**20),
    )(early, early_other, band, band_other, master, cols, table)


def last_weights(late, late_other, spread, table, started):
    return pl.pallas_call(
        last_weights_kernel,
        out_shape=FULL,
        in_specs=[VMEM] * 4 + [ANYWHERE],
        out_specs=ANYWHERE,
        input_output_aliases={4: 0},
        scratch_shapes=[pltpu.VMEM((QUARTER, 16 * GROUP), bf16), pltpu.SemaphoreType.DMA],
        compiler_params=pltpu.CompilerParams(vmem_limit_bytes=12 * 2**20),
    )(late, late_other, spread, table, started)


def send(array, axis, perm):
    return lax.ppermute(array, axis, perm)


together = lax.optimization_barrier


def both(own, got):
    return own.astype(f32) + got.astype(f32)


def all_four(own, axis):
    across, below, above = (send(own, axis, perm) for perm in (ACROSS4, UP4, DOWN4))
    return lambda: both(own, across) + both(below, above)


def local(gradients, momentum, master_weights):
    table = cosine_rows()
    mom = momentum[0]
    half = (ROWS, GROUP)
    z = ("zl", "zh")

    sent, own = split_blocks(gradients[0, 0])
    other = send(sent, "core", SWAP2)
    w0 = small_call(cast_kernel, jax.ShapeDtypeStruct((QUARTER, GROUP), bf16), master_weights)
    wz = send(w0, z, CROSS8)
    up, down, keep_up, keep_down, mine, band = pair_sum(
        own,
        other,
        mom,
        jnp.asarray(np.tile(table.T, (1, 8)), f32),
        jnp.asarray(table, f32),
    )

    band = band.astype(bf16)
    got = send(band, "zl", EVEN4)
    up, down = enclosed(w0, wz, up, down)
    left = send(up, "x", UP4)
    right = send(down, "x", DOWN4)

    total = all_four(both(band, got).astype(bf16), "y")

    band = total().astype(bf16)
    got = send(band, "zl", XOR2)

    band, left, right = together((both(band, got), left, right))
    band = band.astype(bf16)
    got = send(band, z, CROSS8)
    passed = jax.ShapeDtypeStruct((2 * HALF + QUARTER, GROUP), bf16)
    up, down = small_call(pass_on_kernel, [passed] * 2, keep_up, keep_down, left, right)
    last_left = send(up, "x", UP4)
    last_right = send(down, "x", DOWN4)

    band, last_left, last_right = together((both(band, got), last_left, last_right))
    total = all_four(band.astype(bf16), "x")
    parts = (mine, left, right, last_left, last_right)
    eighth = small_call(
        collect_kernel, jax.ShapeDtypeStruct((8, QUARTER, GROUP), bf16), w0, wz, *parts[1:]
    )
    below = send(eighth, "y", UP4)
    above = send(eighth, "y", DOWN4)
    z_send = small_call(z_send_kernel, jax.ShapeDtypeStruct(half, bf16), *parts)
    from_z = send(z_send, "zh", SWAP2)

    band, eighth, below, above, from_z = together((total(), eighth, below, above, from_z))
    band = (band * (-step_size / replicas)).astype(bf16)
    band_other = send(band, "core", SWAP2)
    early = packed(eighth, below, above)
    early_other = send(early, "core", SWAP2)
    four = jax.ShapeDtypeStruct((4, QUARTER, GROUP), bf16)
    up, down = small_call(half_kernel, [four] * 2, below, above)
    low = send(up, "y", UP4)
    high = send(down, "y", DOWN4)
    columns_table = jnp.asarray(np.tile(table, (8, 1)), f32)
    new_master, started, spread = first_weights(
        early,
        early_other,
        band,
        band_other,
        master_weights,
        jnp.asarray(np.kron(np.eye(8), table.T), bf16),
        columns_table,
    )
    new_momentum = small_call(
        remaining_kernel,
        jax.ShapeDtypeStruct(half, f32),
        *parts,
        from_z,
        mom,
        jnp.asarray(table.T @ table, f32),
    )

    spread, new_momentum, low, high = together((spread, new_momentum, low, high))
    late = packed(low, high)
    late_other = send(late, "core", SWAP2)
    weights_full = last_weights(late, late_other, spread, columns_table, started)
    return (new_momentum[None], new_master, weights_full)


def solution(mesh):
    fine = Mesh(mesh.devices.reshape(4, 4, 4, 2, 2), ("y", "zl", "x", "zh", "core"))
    rep, fsdp = ("y", "zl"), ("x", "zh", "core")
    return jax.shard_map(
        local,
        mesh=fine,
        in_specs=(P(rep, fsdp, None, None), P(rep, None, fsdp), P(None, fsdp)),
        out_specs=(P(rep, None, fsdp), P(None, fsdp), P()),
        check_vma=False,
    )
```

```python
import functools

import jax
import jax.numpy as jnp
import numpy as np
from jax import lax
from jax.experimental import pallas as pl
from jax.experimental.pallas import tpu as pltpu
from jax.sharding import Mesh
from jax.sharding import PartitionSpec as P

GROUP = 128
BAND = 16
ROWS = 1024
HALF = 512
QUARTER = 256

momentum_decay = 0.9
step_size = 0.05
replicas = 16

bf16 = jnp.bfloat16
f32 = jnp.float32
HIGHEST = lax.Precision.HIGHEST

SWAP2 = [(0, 1), (1, 0)]
UP4 = [(i, (i + 1) % 4) for i in range(4)]
DOWN4 = [(i, (i + 3) % 4) for i in range(4)]
ACROSS4 = [(i, (i + 2) % 4) for i in range(4)]
EVEN4 = [(0, 1), (1, 0), (2, 3), (3, 2)]
ODD4 = [(1, 2), (2, 1), (3, 0), (0, 3)]
XOR2 = [(i, i ^ 2) for i in range(4)]
CROSS8 = [(i, i ^ 5) for i in range(8)]


def cosine_rows():
    freq = np.arange(BAND, dtype=np.float64)[:, None]
    place = np.arange(GROUP, dtype=np.float64)[None, :]
    factor = np.where(freq == 0.0, np.sqrt(1.0 / GROUP), np.sqrt(2.0 / GROUP))
    return factor * np.cos(np.pi * (2.0 * place + 1.0) * freq / (2.0 * GROUP))


def column_of(dx, gz, core):
    bx = lax.rem(lax.axis_index("x") + dx, 4)
    zh = lax.axis_index("zh")
    bz = zh if gz == 0 else 1 - zh
    return bx * 4 + bz * 2 + core


def slot_of(dx, gz):
    bx = lax.rem(lax.axis_index("x") + dx, 4)
    zh = lax.axis_index("zh")
    return bx * 2 + (zh if gz == 0 else 1 - zh)


def lanes(index):
    return pl.ds(pl.multiple_of(index * GROUP, GROUP), GROUP)


def split_kernel(g_ref, sent_ref, own_ref):
    core = lax.axis_index("core")
    for gz in range(2):
        for dx in range(4):
            k = gz * 4 + dx
            sent_ref[k] = g_ref[:, lanes(column_of(dx, gz, 1 - core))]
            own_ref[k] = g_ref[:, lanes(column_of(dx, gz, core))]


def split_blocks(g):
    blocks = jax.ShapeDtypeStruct((8, ROWS, GROUP), bf16)
    return pl.pallas_call(
        split_kernel,
        out_shape=[blocks, blocks],
        in_specs=[pl.BlockSpec(memory_space=pltpu.VMEM)],
        out_specs=[pl.BlockSpec(memory_space=pltpu.VMEM)] * 2,
        compiler_params=pltpu.CompilerParams(vmem_limit_bytes=12 * 2**20),
    )(g)


def pair_sum_kernel(
    own_ref, other_ref, mom_ref, table_ref, rows_ref, up_ref, down_ref, keep_up_ref, keep_down_ref,
    mine_ref, band_ref, acc_ref,
):
    lane_slot = lax.broadcasted_iota(jnp.int32, (GROUP, GROUP), 1) // BAND
    table = table_ref[...]
    zero = jnp.zeros_like(table)
    for gz in range(2):
        for dx in range(4):
            k = gz * 4 + dx
            s = (own_ref[k].astype(f32) + other_ref[k].astype(f32)).astype(bf16)
            if dx == 0:
                mine_ref[gz] = s
            elif dx == 1:
                keep_up_ref[gz] = s[:HALF]
                up_ref[gz * 2 + 1] = s[HALF:]
            elif dx == 2:
                up_ref[gz * 2] = s[:HALF]
                down_ref[gz * 2] = s[HALF:]
            else:
                down_ref[gz * 2 + 1] = s[:HALF]
                keep_down_ref[gz] = s[HALF:]
            placed = jnp.where(lane_slot == slot_of(dx, gz), table, zero)
            part = jnp.dot(s, placed.astype(bf16), preferred_element_type=f32)
            if k == 0:
                acc_ref[...] = part + jnp.dot(
                    momentum_decay * mom_ref[...], placed, preferred_element_type=f32
                )
            else:
                acc_ref[...] += part
    for a in range(ROWS // GROUP):
        band_ref[a * BAND : (a + 1) * BAND, :] = jnp.dot(
            rows_ref[...],
            acc_ref[a * GROUP : (a + 1) * GROUP, :],
            precision=HIGHEST,
            preferred_element_type=f32,
        )


def pair_sum(*args):
    shapes = [(5, HALF, GROUP)] * 2 + [(2, HALF, GROUP)] * 2 + [(2, ROWS, GROUP)]
    shapes = [jax.ShapeDtypeStruct(shape, bf16) for shape in shapes]
    shapes.append(jax.ShapeDtypeStruct((ROWS // GROUP * BAND, GROUP), f32))
    vmem = pl.BlockSpec(memory_space=pltpu.VMEM)
    return pl.pallas_call(
        pair_sum_kernel,
        out_shape=shapes,
        in_specs=[vmem] * 5,
        out_specs=[vmem] * 6,
        scratch_shapes=[pltpu.VMEM((ROWS, GROUP), f32)],
        compiler_params=pltpu.CompilerParams(vmem_limit_bytes=16 * 2**20),
    )(*args)


def small_call(kernel, shapes, *args, cost=None):
    vmem = pl.BlockSpec(memory_space=pltpu.VMEM)
    return pl.pallas_call(
        kernel,
        out_shape=shapes,
        in_specs=[vmem] * len(args),
        out_specs=jax.tree.map(lambda _: vmem, shapes),
        cost_estimate=cost,
        compiler_params=pltpu.CompilerParams(vmem_limit_bytes=8 * 2**20),
    )(*args)


def join_kernel(first_ref, second_ref, out_ref):
    half = first_ref.shape[0]
    out_ref[:half] = first_ref[...]
    out_ref[half:] = second_ref[...]


def joined(first, second):
    shape = (2 * first.shape[0], *first.shape[1:])
    return small_call(join_kernel, jax.ShapeDtypeStruct(shape, first.dtype), first, second)


def cast_kernel(master_ref, out_ref):
    y = lax.axis_index("y")
    out_ref[...] = master_ref[pl.ds(pl.multiple_of(y * QUARTER, QUARTER), QUARTER), :].astype(bf16)


def enclose_kernel(w0_ref, wz_ref, up_in_ref, down_in_ref, up_ref, down_ref):
    del up_in_ref, down_in_ref
    for ref in (up_ref, down_ref):
        ref[4, :QUARTER] = w0_ref[...]
        ref[4, QUARTER:] = wz_ref[...]


def enclosed(w0, wz, up, down):
    vmem = pl.BlockSpec(memory_space=pltpu.VMEM)
    return pl.pallas_call(
        enclose_kernel,
        out_shape=[jax.ShapeDtypeStruct(up.shape, bf16)] * 2,
        in_specs=[vmem] * 4,
        out_specs=[vmem] * 2,
        input_output_aliases={2: 0, 3: 1},
        compiler_params=pltpu.CompilerParams(vmem_limit_bytes=8 * 2**20),
    )(w0, wz, up, down)


def pass_on_kernel(keep_up_ref, keep_down_ref, left_ref, right_ref, up_ref, down_ref):
    for gz in range(2):
        r = slice(gz * HALF, (gz + 1) * HALF)
        up_ref[r] = (keep_up_ref[gz].astype(f32) + left_ref[gz * 2].astype(f32)).astype(bf16)
        down_ref[r] = (keep_down_ref[gz].astype(f32) + right_ref[gz * 2].astype(f32)).astype(bf16)
    up_ref[2 * HALF :] = left_ref[4, :QUARTER]
    down_ref[2 * HALF :] = right_ref[4, QUARTER:]


def collect_kernel(w0_ref, wz_ref, left_ref, right_ref, last_left_ref, last_right_ref, out_ref):
    out_ref[0] = w0_ref[...]
    out_ref[1] = left_ref[4, :QUARTER]
    out_ref[2] = right_ref[4, :QUARTER]
    out_ref[3] = last_left_ref[2 * HALF :]
    out_ref[4] = wz_ref[...]
    out_ref[5] = left_ref[4, QUARTER:]
    out_ref[6] = right_ref[4, QUARTER:]
    out_ref[7] = last_right_ref[2 * HALF :]


def half_kernel(below_ref, above_ref, low_ref, high_ref):
    low_ref[...] = below_ref[:4]
    high_ref[...] = above_ref[4:]


def pack_kernel(*refs):
    at = 0
    for ref in refs[:-1]:
        refs[-1][at : at + ref.shape[0]] = ref[...]
        at += ref.shape[0]


def packed(*parts):
    blocks = sum(part.shape[0] for part in parts)
    return small_call(pack_kernel, jax.ShapeDtypeStruct((blocks, QUARTER, GROUP), bf16), *parts)


def x_total(mine_ref, left_ref, right_ref, last_left_ref, last_right_ref, gz, a):
    r = slice(a * GROUP, (a + 1) * GROUP)
    h = slice(a % 4 * GROUP, (a % 4 + 1) * GROUP)
    p = slice(gz * HALF + a % 4 * GROUP, gz * HALF + (a % 4 + 1) * GROUP)
    direct, passed = (right_ref, last_left_ref) if a < 4 else (left_ref, last_right_ref)
    total = mine_ref[gz, r].astype(f32) + direct[gz * 2 + 1, h].astype(f32)
    return total + passed[p].astype(f32)


def z_send_kernel(*refs):
    for a in range(ROWS // GROUP):
        refs[5][a * GROUP : (a + 1) * GROUP] = x_total(*refs[:5], 1, a).astype(bf16)


def remaining_kernel(*refs):
    z_ref, mom_ref, q_ref, out_ref = refs[5:]
    q = q_ref[...]
    for a in range(ROWS // GROUP):
        r = slice(a * GROUP, (a + 1) * GROUP)
        summed = x_total(*refs[:5], 0, a) + z_ref[r].astype(f32)
        moment = momentum_decay * mom_ref[r] + summed
        low = jnp.dot(moment, q, preferred_element_type=f32)
        low = jnp.dot(q, low, preferred_element_type=f32)
        out_ref[r] = moment - low


def columns_side(table_ref):
    x, zh = lax.axis_index("x"), lax.axis_index("zh")
    row_slot = lax.broadcasted_iota(jnp.int32, (GROUP, GROUP), 0) // BAND
    table = table_ref[...]
    zero = jnp.zeros_like(table)
    columns = []
    wide = []
    for gz in range(2):
        for dx in (0, 3, 1, 2):
            bx, bz = lax.rem(x + dx, 4), (zh if gz == 0 else 1 - zh)
            columns.append(bx * 4 + bz * 2)
            wide.append(jnp.where(row_slot == bx * 2 + bz, table, zero).astype(bf16))
    return jnp.concatenate(wide, axis=1), columns


def update_quarter(dy, packs, at, spread_ref, wide, columns, page_ref, full_out, sem):
    core = lax.axis_index("core")
    quarter = lax.rem(lax.axis_index("y") + dy, 4)
    rows = pl.ds(pl.multiple_of(quarter * QUARTER, QUARTER), QUARTER)
    for who in range(2):
        side = core if who == 0 else 1 - core
        update = jnp.dot(
            spread_ref[rows, who * GROUP : (who + 1) * GROUP], wide, preferred_element_type=f32
        )
        for k, column in enumerate(columns):
            new = packs[who][at + k].astype(f32) + update[:, k * GROUP : (k + 1) * GROUP]
            page_ref[:, lanes(column + side)] = new.astype(bf16)
    copy = pltpu.make_async_copy(page_ref, full_out.at[rows, :], sem)
    copy.start()
    return copy


def first_weights_kernel(
    early_ref, early_other_ref, band_ref, band_other_ref, master_ref, cols_ref, table_ref,
    master_out, full_out, spread_ref, page_ref, sem,
):
    wide, columns = columns_side(table_ref)
    coeffs = jnp.concatenate([band_ref[...], band_other_ref[...]], axis=1)
    spread_ref[...] = jnp.dot(
        cols_ref[...], coeffs, preferred_element_type=f32
    ).astype(bf16)
    packs = (early_ref, early_other_ref)
    copies = [
        update_quarter(
            dy, packs, 8 * step, spread_ref, wide, columns, page_ref.at[step], full_out, sem.at[step]
        )
        for step, dy in enumerate((0, 3, 1))
    ]
    master_out[...] = master_ref[...] + jnp.dot(
        spread_ref[:, :GROUP], wide[:, :GROUP], preferred_element_type=f32
    )
    for copy in copies:
        copy.wait()


def last_weights_kernel(
    late_ref, late_other_ref, spread_ref, table_ref, started_ref, full_out, page_ref, sem
):
    del started_ref
    wide, columns = columns_side(table_ref)
    packs = (late_ref, late_other_ref)
    update_quarter(2, packs, 0, spread_ref, wide, columns, page_ref, full_out, sem).wait()


VMEM = pl.BlockSpec(memory_space=pltpu.VMEM)
ANYWHERE = pl.BlockSpec(memory_space=pl.ANY)
FULL = jax.ShapeDtypeStruct((ROWS, 16 * GROUP), bf16)


def first_weights(early, early_other, band, band_other, master, cols, table):
    return pl.pallas_call(
        first_weights_kernel,
        out_shape=[
            jax.ShapeDtypeStruct((ROWS, GROUP), f32),
            FULL,
            jax.ShapeDtypeStruct((ROWS, 2 * GROUP), bf16),
        ],
        in_specs=[VMEM] * 7,
        out_specs=[VMEM, ANYWHERE, VMEM],
        scratch_shapes=[
            pltpu.VMEM((3, QUARTER, 16 * GROUP), bf16),
            pltpu.SemaphoreType.DMA((3,)),
        ],
        compiler_params=pltpu.CompilerParams(vmem_limit_bytes=20 * 2**20),
    )(early, early_other, band, band_other, master, cols, table)


def last_weights(late, late_other, spread, table, started):
    return pl.pallas_call(
        last_weights_kernel,
        out_shape=FULL,
        in_specs=[VMEM] * 4 + [ANYWHERE],
        out_specs=ANYWHERE,
        input_output_aliases={4: 0},
        scratch_shapes=[pltpu.VMEM((QUARTER, 16 * GROUP), bf16), pltpu.SemaphoreType.DMA],
        compiler_params=pltpu.CompilerParams(vmem_limit_bytes=12 * 2**20),
    )(late, late_other, spread, table, started)


def send(array, axis, perm):
    return lax.ppermute(array, axis, perm)


together = lax.optimization_barrier


def both(own, got):
    return own.astype(f32) + got.astype(f32)


def all_four(own, axis):
    across, below, above = (send(own, axis, perm) for perm in (ACROSS4, UP4, DOWN4))
    return lambda: both(own, across) + both(below, above)


def local(gradients, momentum, master_weights):
    table = cosine_rows()
    mom = momentum[0]
    half = (ROWS, GROUP)
    z = ("zl", "zh")

    sent, own = split_blocks(gradients[0, 0])
    other = send(sent, "core", SWAP2)
    w0 = small_call(cast_kernel, jax.ShapeDtypeStruct((QUARTER, GROUP), bf16), master_weights)
    wz = send(w0, z, CROSS8)
    up, down, keep_up, keep_down, mine, band = pair_sum(
        own,
        other,
        mom,
        jnp.asarray(np.tile(table.T, (1, 8)), f32),
        jnp.asarray(table, f32),
    )

    band = band.astype(bf16)
    got = send(band, "zl", EVEN4)
    up, down = enclosed(w0, wz, up, down)
    left = send(up, "x", UP4)
    right = send(down, "x", DOWN4)

    total = all_four(both(band, got).astype(bf16), "y")

    band = total().astype(bf16)
    got = send(band, "zl", XOR2)

    band, left, right = together((both(band, got), left, right))
    band = band.astype(bf16)
    got = send(band, z, CROSS8)
    passed = jax.ShapeDtypeStruct((2 * HALF + QUARTER, GROUP), bf16)
    up, down = small_call(pass_on_kernel, [passed] * 2, keep_up, keep_down, left, right)
    last_left = send(up, "x", UP4)
    last_right = send(down, "x", DOWN4)

    band, last_left, last_right = together((both(band, got), last_left, last_right))
    total = all_four(band.astype(bf16), "x")
    parts = (mine, left, right, last_left, last_right)
    eighth = small_call(
        collect_kernel, jax.ShapeDtypeStruct((8, QUARTER, GROUP), bf16), w0, wz, *parts[1:]
    )
    below = send(eighth, "y", UP4)
    above = send(eighth, "y", DOWN4)
    z_send = small_call(z_send_kernel, jax.ShapeDtypeStruct(half, bf16), *parts)
    from_z = send(z_send, "zh", SWAP2)

    band, eighth, below, above, from_z = together((total(), eighth, below, above, from_z))
    band = (band * (-step_size / replicas)).astype(bf16)
    band_other = send(band, "core", SWAP2)
    early = packed(eighth, below, above)
    early_other = send(early, "core", SWAP2)
    four = jax.ShapeDtypeStruct((4, QUARTER, GROUP), bf16)
    up, down = small_call(half_kernel, [four] * 2, below, above)
    low = send(up, "y", UP4)
    high = send(down, "y", DOWN4)
    columns_table = jnp.asarray(np.tile(table, (8, 1)), f32)
    new_master, started, spread = first_weights(
        early,
        early_other,
        band,
        band_other,
        master_weights,
        jnp.asarray(np.kron(np.eye(8), table.T), bf16),
        columns_table,
    )
    new_momentum = small_call(
        remaining_kernel,
        jax.ShapeDtypeStruct(half, f32),
        *parts,
        from_z,
        mom,
        jnp.asarray(table.T @ table, f32),
    )

    spread, new_momentum, low, high = together((spread, new_momentum, low, high))
    late = packed(low, high)
    late_other = send(late, "core", SWAP2)
    weights_full = last_weights(late, late_other, spread, columns_table, started)
    return (new_momentum[None], new_master, weights_full)


def solution(mesh):
    fine = Mesh(mesh.devices.reshape(4, 4, 4, 2, 2), ("y", "zl", "x", "zh", "core"))
    rep, fsdp = ("y", "zl"), ("x", "zh", "core")
    return jax.shard_map(
        local,
        mesh=fine,
        in_specs=(P(rep, fsdp, None, None), P(rep, None, fsdp), P(None, fsdp)),
        out_specs=(P(rep, None, fsdp), P(None, fsdp), P()),
        check_vma=False,
    )
```
